512 devices in a mesh: row: 16 (over z), col: 8 (over x_lo, y), depth: 4 (over x_hi, core).
Axes of the slice: x: 4 (x_hi: 2, x_lo: 2; x = x_hi * 2 + x_lo), y: 4, z: 16, core: 2. Of those that a mesh axis runs over, the one named last changes fastest.
Arguments:
- h_blocks: bfloat16 [16, 16, 4, 12, 128, 128], P('row', 'col', 'depth'), may hold values from -0.25 to 0.25
- h_rows: int32 [16, 16, 4, 12], P('row', 'col', 'depth'), may hold values from 0 to 31, as said below
- h_cols: int32 [16, 16, 4, 12], P('row', 'col', 'depth'), may hold values from 0 to 7
- h_flags: int32 [16, 16, 4, 12], P('row', 'col', 'depth'), may hold values from 0 to 1
- x_blocks: bfloat16 [16, 4, 8, 8, 2, 128, 128], P('row', 'depth', 'col'), may hold values from -6 to 6
- x_cols: int32 [16, 4, 8, 8, 2], P('row', 'depth', 'col'), may hold values from 0 to 7, as said below
- x_flags: int32 [16, 4, 8, 8, 2], P('row', 'depth', 'col'), may hold values from 0 to 1
- previous: bfloat16 [16, 4, 8, 8, 2, 128, 128], P('row', 'depth', 'col'), may hold values from -6 to 6
Outputs:
- next_term: bfloat16 [16, 4, 8, 8, 2, 128, 128], P('row', 'depth', 'col')
The draws below stay inside these ranges and needn't reach their ends.
Inputs may be any that keep to these rules, and one draw needn't show every extreme that they name: The slots of one tile (g, p, e) name distinct positions (h_rows, h_cols); live slots come first; every tile with g = p has all 12 slots live. `x_cols`: the 2 slots of one block row in one column group name distinct columns.
All inputs are finite; a program needn't handle non-finite values.
Results may differ from the reference program's by a relative error of at most 0.0095.
Values may be sent and summed in bfloat16 or wider, within the bound.
No kernel may reach another device: no remote copies, remote signals or barrier semaphores. Data moves between devices by JAX's collectives and lax.ppermute only.
A program may use at most 64 MiB of HBM per device.

```python
import jax
import jax.numpy as jnp
from jax import lax

BLOCK = 128
HAM_SLOTS = 12
ITER_SLOTS = 2
COL_BLOCKS = 8
GROUP_ROWS = 32
PIECE_ROWS = 8
N_ROW = 16
N_COL = 8
N_DEPTH = 4


def hamiltonian_pattern(key):
    key = jax.random.fold_in(key, 11)
    keys = jax.random.split(key, 4)
    tiles = (N_ROW, N_ROW, N_DEPTH)
    spots = GROUP_ROWS * PIECE_ROWS
    scores = jax.random.randint(keys[0], tiles + (spots,), 0, max(1, (1 << 30) // spots))
    scores = scores * spots + jnp.arange(spots, dtype=jnp.int32)
    _, places = lax.top_k(scores, HAM_SLOTS)
    places = places.astype(jnp.int32)
    ham_rows = places // PIECE_ROWS
    ham_cols = places % PIECE_ROWS
    far_count = jax.random.randint(keys[1], tiles, 0, HAM_SLOTS + 1)
    far_count = far_count * (jax.random.randint(keys[2], tiles, 0, 4) == 0).astype(jnp.int32)
    near_count = jax.random.randint(keys[3], tiles, HAM_SLOTS // 2, HAM_SLOTS + 1)
    group_index = jnp.arange(N_ROW, dtype=jnp.int32)[:, None, None]
    piece_index = jnp.arange(N_ROW, dtype=jnp.int32)[None, :, None]
    distance = jnp.abs(group_index - piece_index)
    count = jnp.where(distance == 0, HAM_SLOTS, jnp.where(distance == 1, near_count, far_count))
    ham_flags = (jnp.arange(HAM_SLOTS, dtype=jnp.int32)[None, None, None, :] < count[..., None]).astype(jnp.int32)
    return (ham_rows, ham_cols, ham_flags)


def iterate_pattern(key):
    key = jax.random.fold_in(key, 23)
    keys = jax.random.split(key, 4)
    shape = (N_ROW, N_DEPTH, N_COL, PIECE_ROWS)
    first = jax.random.randint(keys[0], shape, 0, COL_BLOCKS)
    stride = jax.random.randint(keys[1], shape, 1, COL_BLOCKS // ITER_SLOTS + 1)
    offsets = jnp.arange(ITER_SLOTS, dtype=jnp.int32)
    iter_cols = (first[..., None] + offsets * stride[..., None]) % COL_BLOCKS
    live = jax.random.randint(keys[2], shape + (ITER_SLOTS,), 0, 2)
    full_row = jax.random.randint(keys[3], (N_ROW, N_DEPTH, N_COL), 0, PIECE_ROWS)
    is_full = jnp.arange(PIECE_ROWS, dtype=jnp.int32)[None, None, None, :] == full_row[..., None]
    iter_flags = jnp.where(is_full[..., None], 1, live).astype(jnp.int32)
    return (iter_cols.astype(jnp.int32), iter_flags)


def draw_h_rows(key, part):
    return hamiltonian_pattern(key)[0]


def draw_h_cols(key, part):
    return hamiltonian_pattern(key)[1]


def draw_h_flags(key, part):
    return hamiltonian_pattern(key)[2]


def draw_x_cols(key, part):
    return iterate_pattern(key)[0]


def draw_x_flags(key, part):
    return iterate_pattern(key)[1]


def level_of(key, shape, cuts, smallest, largest):
    gain = 1.0
    for axis_at, parts in cuts:
        draws = jax.random.uniform(jax.random.fold_in(jax.random.fold_in(key, 6), axis_at), (parts,), jnp.float32, smallest / len(cuts), largest / len(cuts))
        gain = gain * jnp.repeat(jnp.exp(draws), shape[axis_at] // parts).reshape((-1,) + (1,) * (len(shape) - 1 - axis_at))
    return gain


def scatter_about(rng, shape, spread, limit, shards=(), kind=jnp.bfloat16):
    factor_of = level_of(rng, shape, shards, -0.22, 0.18) if shards else 1.0
    drawn = jax.random.normal(rng, shape, jnp.float32) * spread * factor_of
    return jnp.minimum(jnp.maximum(drawn, -limit), limit).astype(kind)


def setup_inputs(seed: int = 0) -> dict:
    streams_of = jax.random.split(jax.random.key(seed), 9)
    return {
        "h_blocks": scatter_about(streams_of[0], (N_ROW, N_ROW, N_DEPTH, HAM_SLOTS, BLOCK, BLOCK), (4 * BLOCK) ** -0.5, 0.25, ((0, 16), (1, 8), (2, 4))),
        "h_rows": draw_h_rows(jax.random.fold_in(streams_of[8], 71), 0),
        "h_cols": draw_h_cols(jax.random.fold_in(streams_of[8], 71), 0),
        "h_flags": draw_h_flags(jax.random.fold_in(streams_of[8], 71), 0),
        "x_blocks": scatter_about(streams_of[4], (N_ROW, N_DEPTH, N_COL, PIECE_ROWS, ITER_SLOTS, BLOCK, BLOCK), 1.0, 6.0, ((0, 16), (1, 4), (2, 8))),
        "x_cols": draw_x_cols(jax.random.fold_in(streams_of[8], 71), 0),
        "x_flags": draw_x_flags(jax.random.fold_in(streams_of[8], 71), 0),
        "previous": scatter_about(streams_of[7], (N_ROW, N_DEPTH, N_COL, PIECE_ROWS, ITER_SLOTS, BLOCK, BLOCK), 1.0, 6.0, ((0, 16), (1, 4), (2, 8))),
    }


def reference(h_blocks, h_rows, h_cols, h_flags, x_blocks, x_cols, x_flags, previous):
    def row_group(group):
        aim_cols = jnp.swapaxes(x_cols[group], 0, 1).reshape(N_COL, GROUP_ROWS, ITER_SLOTS)
        aim_flags = jnp.swapaxes(x_flags[group], 0, 1).reshape(N_COL, GROUP_ROWS, ITER_SLOTS)
        summed = jnp.zeros((N_COL, GROUP_ROWS * ITER_SLOTS, BLOCK, BLOCK), jnp.float32)
        for depth_index in range(N_DEPTH):
            def one_piece(running, piece):
                blocks = h_blocks[group, piece, depth_index].astype(jnp.float32)
                ham_rows = h_rows[group, piece, depth_index]
                ham_cols = h_cols[group, piece, depth_index]
                ham_flags = h_flags[group, piece, depth_index]
                picked = jnp.take(x_blocks[piece, depth_index], ham_cols, axis=1).astype(jnp.float32)
                picked_cols = jnp.take(x_cols[piece, depth_index], ham_cols, axis=1)
                picked_flags = jnp.take(x_flags[piece, depth_index], ham_cols, axis=1)
                wanted_cols = jnp.take(aim_cols, ham_rows, axis=1)
                wanted_flags = jnp.take(aim_flags, ham_rows, axis=1)
                paired = picked_cols[:, :, :, None] == wanted_cols[:, :, None, :]
                paired = paired & (picked_flags[:, :, :, None] > 0) & (wanted_flags[:, :, None, :] > 0)
                paired = paired & (ham_flags[None, :, None, None] > 0)
                products = jnp.einsum("akl,cawlm->cawkm", blocks, picked)
                terms = jnp.einsum("cawv,cawkm->cavkm", paired.astype(jnp.float32), products)
                target = ham_rows[:, None] * ITER_SLOTS + jnp.arange(ITER_SLOTS, dtype=jnp.int32)[None, :]
                target = target.reshape(-1).astype(jnp.int32)
                running = running.at[:, target].add(terms.reshape((N_COL, -1, BLOCK, BLOCK)))
                return running, None

            start_sum = jnp.zeros((N_COL, GROUP_ROWS * ITER_SLOTS, BLOCK, BLOCK), jnp.float32)
            partial_sum, _ = lax.scan(one_piece, start_sum, jnp.arange(N_ROW, dtype=jnp.int32))
            rounded = lax.optimization_barrier(partial_sum.astype(jnp.bfloat16))
            summed = summed + rounded.astype(jnp.float32)
        summed = summed.reshape(N_COL, N_DEPTH, PIECE_ROWS, ITER_SLOTS, BLOCK, BLOCK)
        summed = jnp.transpose(summed, (1, 0, 2, 3, 4, 5))
        prior = previous[group].astype(jnp.float32)
        live = x_flags[group].astype(jnp.float32)[..., None, None]
        return ((2.0 * summed - prior) * live).astype(jnp.bfloat16)

    return lax.map(row_group, jnp.arange(N_ROW, dtype=jnp.int32))
```

```python
import jax
import jax.numpy as jnp
from jax import lax
from jax.experimental import pallas as pl
from jax.experimental.pallas import tpu as pltpu
from jax.sharding import PartitionSpec as P

WINDOW = 16


def pair_kernel(where, ham, iterate, aim, pairs):
    cols, width = ham.shape[0], iterate.shape[1] // 2
    slots = ham.shape[1] // 3
    per_tile = slots // (iterate.shape[0] // cols)
    near = where[0] // 4
    step = where[0] % 4

    def one_slot(at, count):
        col = at // slots
        slot = at % slots
        row = ham[col, slot]
        inner = ham[col, slots + slot]
        live = ham[col, 2 * slots + slot] > 0
        piece = col * (slots // per_tile) + slot // per_tile
        array = ((col // 4) ^ near) * 4 + (step - col % 4 + 4) % 4
        owner = row // 8
        for w in range(2):
            spot = inner * 2 + w
            there = iterate[piece, spot]
            on = live & (iterate[piece, width + spot] > 0)
            for v in range(2):
                place = (row % 8) * 2 + v
                match = on & (aim[owner, place] == there) & (aim[owner, width + place] > 0)
                pairs[count] = (array * slots + slot) + (piece * width + spot) * 256 + (row * 2 + v) * 65536
                count = count + match.astype(jnp.int32)
        return count

    pairs[pairs.shape[0] - 1] = lax.fori_loop(0, cols * slots, one_slot, jnp.int32(0))


def product_kernel(pairs, where, iterate, *rest):
    hams, (sent, kept, total, ham_buf, it_buf, ham_sem, it_sem) = rest[:8], rest[8:]
    slots = hams[0].shape[0]
    count = pairs[pairs.shape[0] - 1]

    def start(at):
        code = pairs[at]
        ham_at = code % 256
        slot = at % WINDOW
        for k, ham in enumerate(hams):

            @pl.when(ham_at // slots == k)
            def _():
                pltpu.make_async_copy(ham.at[ham_at % slots], ham_buf.at[slot], ham_sem.at[slot]).start()

        pltpu.make_async_copy(iterate.at[(code // 256) % 256], it_buf.at[slot], it_sem.at[slot]).start()

    def first(at, carry):
        start(at)
        return carry

    lax.fori_loop(0, jnp.minimum(count, WINDOW), first, 0)

    def clear(at, carry):
        total[at] = jnp.zeros(total.shape[1:], total.dtype)
        return carry

    lax.fori_loop(0, total.shape[0], clear, 0, unroll=4)

    def multiply(at, carry):
        slot = at % WINDOW
        pltpu.make_async_copy(hams[0].at[0], ham_buf.at[slot], ham_sem.at[slot]).wait()
        pltpu.make_async_copy(iterate.at[0], it_buf.at[slot], it_sem.at[slot]).wait()
        goal = pairs[at] // 65536
        total[goal] += jnp.dot(ham_buf[slot], it_buf[slot], preferred_element_type=jnp.float32)

        @pl.when(at + WINDOW < count)
        def _():
            start(at + WINDOW)

        return carry

    lax.fori_loop(0, count, multiply, 0)
    half = sent.shape[0] // 2
    core = where[1] % 2
    high = where[1] // 2
    for part in range(2):
        target_high = high if part else 1 - high

        def finish(at, carry):
            sent[part * half + at] = total[(target_high * 2 + 1 - core) * half + at].astype(sent.dtype)
            kept[part * half + at] = total[(target_high * 2 + core) * half + at].astype(kept.dtype)
            return carry

        lax.fori_loop(0, half, finish, 0, unroll=2)


def body(h_blocks, h_rows, h_cols, h_flags, x_blocks, x_cols, x_flags, previous):
    block = x_blocks.shape[-1]
    n_row, n_col, n_depth = lax.axis_size("row"), lax.axis_size("col"), lax.axis_size("depth")
    where = jnp.stack([lax.axis_index("col"), lax.axis_index("depth")]).astype(jnp.int32)
    iterate = lax.all_gather(x_blocks[0, 0, 0], "row", axis=0)
    iterate = iterate.reshape(-1, block, block)
    mine = h_blocks[0].reshape(-1, block, block)
    hams = []
    for flip in range(2):
        for step in range(4):
            route = [(c, ((c // 4) ^ flip) * 4 + (c % 4 + step) % 4) for c in range(n_col)]
            hams.append(lax.ppermute(mine, "col", route) if flip or step else mine)
    ham_ints = jnp.concatenate([h_rows.reshape(-1), h_cols.reshape(-1), h_flags.reshape(-1)])
    it_ints = jnp.concatenate([x_cols.reshape(-1), x_flags.reshape(-1)])
    ham_ints = lax.all_gather(ham_ints.reshape(1, 1, -1), "col", axis=0, tiled=True)[:, 0]
    aim_ints = lax.all_gather(it_ints.reshape(1, 1, -1), "depth", axis=0, tiled=True)[:, 0]
    it_ints = lax.all_gather(it_ints.reshape(1, 1, -1), "row", axis=0, tiled=True)[:, 0]
    smem = pl.BlockSpec(memory_space=pltpu.SMEM)
    anywhere = pl.BlockSpec(memory_space=pl.ANY)
    vmem = pl.BlockSpec(memory_space=pltpu.VMEM)
    pairs = pl.pallas_call(
        pair_kernel,
        out_shape=jax.ShapeDtypeStruct((512,), jnp.int32),
        in_specs=[smem] * 4,
        out_specs=smem,
        name="pairs",
    )(where, ham_ints, it_ints, aim_ints)
    results = x_cols.shape[3] * x_cols.shape[4]
    half_shape = jax.ShapeDtypeStruct((2 * results, block, block), jnp.bfloat16)
    sent, kept = pl.pallas_call(
        product_kernel,
        out_shape=(half_shape, half_shape),
        in_specs=[smem, smem] + [anywhere] * 9,
        out_specs=(vmem, vmem),
        scratch_shapes=[
            pltpu.VMEM((n_depth * results, block, block), jnp.float32),
            pltpu.VMEM((WINDOW, block, block), jnp.bfloat16),
            pltpu.VMEM((WINDOW, block, block), jnp.bfloat16),
            pltpu.SemaphoreType.DMA((WINDOW,)),
            pltpu.SemaphoreType.DMA((WINDOW,)),
        ],
        compiler_params=pltpu.CompilerParams(vmem_limit_bytes=24 << 20),
        name="products",
    )(pairs, where, *[pltpu.with_memory_space_constraint(x, pltpu.HBM) for x in (iterate, hams[0])], *hams[1:])
    near = lax.ppermute(sent, "depth", [(d, d ^ 1) for d in range(n_depth)])
    onward = kept[:results].astype(jnp.float32) + near[:results].astype(jnp.float32)
    far = lax.ppermute(onward.astype(jnp.bfloat16), "depth", [(d, d ^ 2) for d in range(n_depth)])
    summed = kept[results:].astype(jnp.float32) + near[results:].astype(jnp.float32)
    summed = summed + far.astype(jnp.float32)
    prior = previous.reshape(results, block, block).astype(jnp.float32)
    live = x_flags.reshape(results, 1, 1).astype(jnp.float32)
    result = (2.0 * summed - prior) * live
    return result.astype(jnp.bfloat16).reshape(previous.shape)


def solution(mesh):
    placed = (
        P("row", "col", "depth", None, None, None),
        P("row", "col", "depth", None),
        P("row", "col", "depth", None),
        P("row", "col", "depth", None),
        P("row", "depth", "col", None, None, None, None),
        P("row", "depth", "col", None, None),
        P("row", "depth", "col", None, None),
        P("row", "depth", "col", None, None, None, None),
    )
    return jax.shard_map(
        body,
        mesh=mesh,
        in_specs=placed,
        out_specs=P("row", "depth", "col", None, None, None, None),
        check_vma=False,
    )
```

```python
import jax
import jax.numpy as jnp
from jax import lax
from jax.experimental import pallas as pl
from jax.experimental.pallas import tpu as pltpu
from jax.sharding import PartitionSpec as P

WINDOW = 16


def pair_kernel(where, ham, iterate, aim, pairs):
    pieces, slots = ham.shape
    per_col = pieces // 8
    width = iterate.shape[1]
    near = where[0] // 4
    step = where[0] % 4

    def one_piece(piece, count):
        col = piece // per_col
        array = ((col // 4) ^ near) * 4 + (step - col % 4 + 4) % 4
        base = (array * per_col + piece % per_col) * slots + piece * width * 256

        def live(state):
            slot, _ = state
            return (slot < slots) & (ham[piece, jnp.minimum(slot, slots - 1)] >= 0)

        def one_slot(state):
            slot, count = state
            key = ham[piece, slot]
            row = key // 8
            inner = key % 8
            for w in range(2):
                there = iterate[piece, inner * 2 + w]
                for v in range(2):
                    pairs[count] = base + slot + (inner * 2 + w) * 256 + (row * 2 + v) * 65536
                    count = count + (aim[row * 2 + v] == there).astype(jnp.int32)
            return slot + 1, count

        return lax.while_loop(live, one_slot, (jnp.int32(0), count))[1]

    pairs[pairs.shape[0] - 1] = lax.fori_loop(0, pieces, one_piece, jnp.int32(0))
    pairs[pairs.shape[0] - 2] = where[1]


def product_kernel(pairs, iterate, *rest):
    hams, (sent, kept, total, ham_buf, it_buf, ham_sem, it_sem) = rest[:8], rest[8:]
    slots = hams[0].shape[0]
    count = pairs[pairs.shape[0] - 1]

    def start(at):
        code = pairs[at]
        ham_at = code % 256
        slot = at % WINDOW
        for k, ham in enumerate(hams):

            @pl.when(ham_at // slots == k)
            def _():
                pltpu.make_async_copy(ham.at[ham_at % slots], ham_buf.at[slot], ham_sem.at[slot]).start()

        pltpu.make_async_copy(iterate.at[(code // 256) % 256], it_buf.at[slot], it_sem.at[slot]).start()

    def first(at, carry):
        start(at)
        return carry

    lax.fori_loop(0, jnp.minimum(count, WINDOW), first, 0)

    def clear(at, carry):
        total[at] = jnp.zeros(total.shape[1:], total.dtype)
        return carry

    lax.fori_loop(0, total.shape[0], clear, 0, unroll=4)

    def multiply(at, carry):
        slot = at % WINDOW
        pltpu.make_async_copy(hams[0].at[0], ham_buf.at[slot], ham_sem.at[slot]).wait()
        pltpu.make_async_copy(iterate.at[0], it_buf.at[slot], it_sem.at[slot]).wait()
        goal = pairs[at] // 65536
        total[goal] += jnp.dot(ham_buf[slot], it_buf[slot], preferred_element_type=jnp.float32)

        @pl.when(at + WINDOW < count)
        def _():
            start(at + WINDOW)

        return carry

    lax.fori_loop(0, count, multiply, 0)
    half = sent.shape[0] // 2
    depth = pairs[pairs.shape[0] - 2]
    core = depth % 2
    high = depth // 2
    for part in range(2):
        target_high = high if part else 1 - high

        def finish(at, carry):
            sent[part * half + at] = total[(target_high * 2 + 1 - core) * half + at].astype(sent.dtype)
            kept[part * half + at] = total[(target_high * 2 + core) * half + at].astype(kept.dtype)
            return carry

        lax.fori_loop(0, half, finish, 0, unroll=2)


def body(h_blocks, h_rows, h_cols, h_flags, x_blocks, x_cols, x_flags, previous):
    block = x_blocks.shape[-1]
    n_row, n_col, n_depth = lax.axis_size("row"), lax.axis_size("col"), lax.axis_size("depth")
    where = jnp.stack([lax.axis_index("col"), lax.axis_index("depth")]).astype(jnp.int32)
    iterate = lax.all_gather(x_blocks[0, 0, 0], "row", axis=0)
    iterate = iterate.reshape(-1, block, block)
    ham_ints = jnp.stack([h_rows, h_cols, h_flags], axis=2)
    ham_ints = lax.all_gather(ham_ints, "col", axis=1, tiled=True)
    it_ints = jnp.concatenate([x_cols, x_flags], axis=2)
    aim_ints = lax.all_gather(it_ints, "depth", axis=1, tiled=True)
    it_ints = lax.all_gather(it_ints, "row", axis=0, tiled=True)
    mine = h_blocks[0].reshape(-1, block, block)
    late, ham_ints, aim_ints, it_ints = lax.optimization_barrier((mine, ham_ints, aim_ints, it_ints))
    hams = []
    for flip in range(2):
        for step in range(n_col // 2):
            route = [(c, ((c // 4) ^ flip) * 4 + (c % 4 + step) % 4) for c in range(n_col)]
            source = late if step % 2 and not flip else mine
            hams.append(lax.ppermute(source, "col", route) if flip or step else mine)
    ham_ints = ham_ints.reshape(-1, 3, ham_ints.shape[-1])
    ham_keys = jnp.where(ham_ints[:, 2] > 0, ham_ints[:, 0] * 8 + ham_ints[:, 1], -1)
    it_keys = jnp.where(it_ints[:, 0, 1] > 0, it_ints[:, 0, 0], -1).reshape(n_row, -1)
    aim_keys = jnp.where(aim_ints[0, :, 1] > 0, aim_ints[0, :, 0], -2).reshape(-1)
    smem = pl.BlockSpec(memory_space=pltpu.SMEM)
    anywhere = pl.BlockSpec(memory_space=pl.ANY)
    vmem = pl.BlockSpec(memory_space=pltpu.VMEM)
    pairs = pl.pallas_call(
        pair_kernel,
        out_shape=jax.ShapeDtypeStruct((512,), jnp.int32),
        in_specs=[smem] * 4,
        out_specs=smem,
        name="pairs",
    )(where, ham_keys, it_keys, aim_keys)
    results = x_cols.shape[3] * x_cols.shape[4]
    half_shape = jax.ShapeDtypeStruct((2 * results, block, block), jnp.bfloat16)
    sent, kept = pl.pallas_call(
        product_kernel,
        out_shape=(half_shape, half_shape),
        in_specs=[smem] + [anywhere] * 9,
        out_specs=(vmem, vmem),
        scratch_shapes=[
            pltpu.VMEM((n_depth * results, block, block), jnp.float32),
            pltpu.VMEM((WINDOW, block, block), jnp.bfloat16),
            pltpu.VMEM((WINDOW, block, block), jnp.bfloat16),
            pltpu.SemaphoreType.DMA((WINDOW,)),
            pltpu.SemaphoreType.DMA((WINDOW,)),
        ],
        compiler_params=pltpu.CompilerParams(vmem_limit_bytes=24 << 20),
        name="products",
    )(*[pltpu.with_memory_space_constraint(x, pltpu.HBM) for x in (pairs, iterate, *hams)])
    near = lax.ppermute(sent, "depth", [(d, d ^ 1) for d in range(n_depth)])
    onward = kept[:results].astype(jnp.float32) + near[:results].astype(jnp.float32)
    far = lax.ppermute(onward.astype(jnp.bfloat16), "depth", [(d, d ^ 2) for d in range(n_depth)])
    summed = kept[results:].astype(jnp.float32) + near[results:].astype(jnp.float32)
    summed = summed + far.astype(jnp.float32)
    prior = previous.reshape(results, block, block).astype(jnp.float32)
    live = x_flags.reshape(results, 1, 1).astype(jnp.float32)
    result = (2.0 * summed - prior) * live
    return result.astype(jnp.bfloat16).reshape(previous.shape)


def solution(mesh):
    placed = (
        P("row", "col", "depth", None, None, None),
        P("row", "col", "depth", None),
        P("row", "col", "depth", None),
        P("row", "col", "depth", None),
        P("row", "depth", "col", None, None, None, None),
        P("row", "depth", "col", None, None),
        P("row", "depth", "col", None, None),
        P("row", "depth", "col", None, None, None, None),
    )
    return jax.shard_map(
        body,
        mesh=mesh,
        in_specs=placed,
        out_specs=P("row", "depth", "col", None, None, None, None),
        check_vma=False,
    )
```

```python
import jax
import jax.numpy as jnp
from jax import lax
from jax.experimental import pallas as pl
from jax.experimental.pallas import tpu as pltpu
from jax.sharding import PartitionSpec as P

WINDOW = 16


def pair_kernel(where, ham, iterate, aim, pairs):
    pieces, slots = ham.shape
    per_col = pieces // 8
    width = iterate.shape[1]
    near = where[0] // 4
    step = where[0] % 4

    def one_piece(piece, count):
        col = piece // per_col
        array = ((col // 4) ^ near) * 4 + (step - col % 4 + 4) % 4
        base = (array * per_col + piece % per_col) * slots + piece * width * 256

        def live(state):
            slot, _ = state
            return (slot < slots) & (ham[piece, jnp.minimum(slot, slots - 1)] >= 0)

        def one_slot(state):
            slot, count = state
            key = ham[piece, slot]
            row = key // 8
            inner = key % 8
            for w in range(2):
                there = iterate[piece, inner * 2 + w]
                for v in range(2):
                    pairs[count] = base + slot + (inner * 2 + w) * 256 + (row * 2 + v) * 65536
                    count = count + (aim[row * 2 + v] == there).astype(jnp.int32)
            return slot + 1, count

        return lax.while_loop(live, one_slot, (jnp.int32(0), count))[1]

    pairs[pairs.shape[0] - 1] = lax.fori_loop(0, pieces, one_piece, jnp.int32(0))
    pairs[pairs.shape[0] - 2] = where[1]


def product_kernel(pairs, iterate, *rest):
    hams, (sent, kept, total, ham_buf, it_buf, ham_sem, it_sem) = rest[:8], rest[8:]
    slots = hams[0].shape[0]
    count = pairs[pairs.shape[0] - 1]

    def start(at):
        code = pairs[at]
        ham_at = code % 256
        slot = at % WINDOW
        for k, ham in enumerate(hams):

            @pl.when(ham_at // slots == k)
            def _():
                pltpu.make_async_copy(ham.at[ham_at % slots], ham_buf.at[slot], ham_sem.at[slot]).start()

        pltpu.make_async_copy(iterate.at[(code // 256) % 256], it_buf.at[slot], it_sem.at[slot]).start()

    def first(at, carry):
        start(at)
        return carry

    lax.fori_loop(0, jnp.minimum(count, WINDOW), first, 0)

    def clear(at, carry):
        total[at] = jnp.zeros(total.shape[1:], total.dtype)
        return carry

    lax.fori_loop(0, total.shape[0], clear, 0, unroll=4)

    def multiply(at, carry):
        slot = at % WINDOW
        pltpu.make_async_copy(hams[0].at[0], ham_buf.at[slot], ham_sem.at[slot]).wait()
        pltpu.make_async_copy(iterate.at[0], it_buf.at[slot], it_sem.at[slot]).wait()
        goal = pairs[at] // 65536
        total[goal] += jnp.dot(ham_buf[slot], it_buf[slot], preferred_element_type=jnp.float32)

        @pl.when(at + WINDOW < count)
        def _():
            start(at + WINDOW)

        return carry

    lax.fori_loop(0, count, multiply, 0)
    half = sent.shape[0] // 2
    depth = pairs[pairs.shape[0] - 2]
    core = depth % 2
    high = depth // 2
    for part in range(2):
        target_high = high if part else 1 - high

        def finish(at, carry):
            sent[part * half + at] = total[(target_high * 2 + 1 - core) * half + at].astype(sent.dtype)
            kept[part * half + at] = total[(target_high * 2 + core) * half + at].astype(kept.dtype)
            return carry

        lax.fori_loop(0, half, finish, 0, unroll=2)


def body(h_blocks, h_rows, h_cols, h_flags, x_blocks, x_cols, x_flags, previous):
    block = x_blocks.shape[-1]
    n_row, n_col, n_depth = lax.axis_size("row"), lax.axis_size("col"), lax.axis_size("depth")
    where = jnp.stack([lax.axis_index("col"), lax.axis_index("depth")]).astype(jnp.int32)
    iterate = lax.all_gather(x_blocks[0, 0, 0], "row", axis=0)
    iterate = iterate.reshape(-1, block, block)
    mine = h_blocks[0].reshape(-1, block, block)
    hams = []
    for flip in range(2):
        for step in range(n_col // 2):
            route = [(c, ((c // 4) ^ flip) * 4 + (c % 4 + step) % 4) for c in range(n_col)]
            hams.append(lax.ppermute(mine, "col", route) if flip or step else mine)
    ham_ints = jnp.stack([h_rows, h_cols, h_flags], axis=2)
    it_ints = jnp.concatenate([x_cols, x_flags], axis=2)
    hams[4], ham_ints, it_ints = lax.optimization_barrier((hams[4], ham_ints, it_ints))
    ham_ints = lax.all_gather(ham_ints, "col", axis=1, tiled=True)
    aim_ints = lax.all_gather(it_ints, "depth", axis=1, tiled=True)
    it_ints = lax.all_gather(it_ints, "row", axis=0, tiled=True)
    ham_ints = ham_ints.reshape(-1, 3, ham_ints.shape[-1])
    ham_keys = jnp.where(ham_ints[:, 2] > 0, ham_ints[:, 0] * 8 + ham_ints[:, 1], -1)
    it_keys = jnp.where(it_ints[:, 0, 1] > 0, it_ints[:, 0, 0], -1).reshape(n_row, -1)
    aim_keys = jnp.where(aim_ints[0, :, 1] > 0, aim_ints[0, :, 0], -2).reshape(-1)
    smem = pl.BlockSpec(memory_space=pltpu.SMEM)
    anywhere = pl.BlockSpec(memory_space=pl.ANY)
    vmem = pl.BlockSpec(memory_space=pltpu.VMEM)
    pairs = pl.pallas_call(
        pair_kernel,
        out_shape=jax.ShapeDtypeStruct((512,), jnp.int32),
        in_specs=[smem] * 4,
        out_specs=smem,
        name="pairs",
    )(where, ham_keys, it_keys, aim_keys)
    results = x_cols.shape[3] * x_cols.shape[4]
    half_shape = jax.ShapeDtypeStruct((2 * results, block, block), jnp.bfloat16)
    sent, kept = pl.pallas_call(
        product_kernel,
        out_shape=(half_shape, half_shape),
        in_specs=[smem] + [anywhere] * 9,
        out_specs=(vmem, vmem),
        scratch_shapes=[
            pltpu.VMEM((n_depth * results, block, block), jnp.float32),
            pltpu.VMEM((WINDOW, block, block), jnp.bfloat16),
            pltpu.VMEM((WINDOW, block, block), jnp.bfloat16),
            pltpu.SemaphoreType.DMA((WINDOW,)),
            pltpu.SemaphoreType.DMA((WINDOW,)),
        ],
        compiler_params=pltpu.CompilerParams(vmem_limit_bytes=24 << 20),
        name="products",
    )(*[pltpu.with_memory_space_constraint(x, pltpu.HBM) for x in (pairs, iterate, *hams)])
    near = lax.ppermute(sent, "depth", [(d, d ^ 1) for d in range(n_depth)])
    onward = kept[:results].astype(jnp.float32) + near[:results].astype(jnp.float32)
    far = lax.ppermute(onward.astype(jnp.bfloat16), "depth", [(d, d ^ 2) for d in range(n_depth)])
    summed = kept[results:].astype(jnp.float32) + near[results:].astype(jnp.float32)
    summed = summed + far.astype(jnp.float32)
    prior = previous.reshape(results, block, block).astype(jnp.float32)
    live = x_flags.reshape(results, 1, 1).astype(jnp.float32)
    result = (2.0 * summed - prior) * live
    return result.astype(jnp.bfloat16).reshape(previous.shape)


def solution(mesh):
    placed = (
        P("row", "col", "depth", None, None, None),
        P("row", "col", "depth", None),
        P("row", "col", "depth", None),
        P("row", "col", "depth", None),
        P("row", "depth", "col", None, None, None, None),
        P("row", "depth", "col", None, None),
        P("row", "depth", "col", None, None),
        P("row", "depth", "col", None, None, None, None),
    )
    return jax.shard_map(
        body,
        mesh=mesh,
        in_specs=placed,
        out_specs=P("row", "depth", "col", None, None, None, None),
        check_vma=False,
    )
```

```python
import jax
import jax.numpy as jnp
from jax import lax
from jax.experimental import pallas as pl
from jax.experimental.pallas import tpu as pltpu
from jax.sharding import PartitionSpec as P

WINDOW = 16


def key_kernel(*refs):
    hams, (keys, slab, sem) = refs[:8], refs[8:]
    tail = slab.shape[1]
    copies = [
        pltpu.make_async_copy(ham.at[pl.ds(ham.shape[0] - tail, tail)], slab.at[k], sem.at[k])
        for k, ham in enumerate(hams)
    ]
    for copy in copies:
        copy.start()
    for k, copy in enumerate(copies):
        copy.wait()
        held = slab[k].astype(jnp.float32)
        place = jnp.where(held[4:6] > 0, held[0:2] * 8 + held[2:4], -1.0)
        keys[2 * k : 2 * k + 2] = place.astype(jnp.int32)


def pair_kernel(where, ham, iterate, aim, pairs):
    pieces = ham.shape[0]
    slots = 12
    per_col = pieces // 8
    width = iterate.shape[1]
    near = where[0] // 4
    step = where[0] % 4

    def one_tile(tile, count):
        array = tile // per_col
        col = ((array // 4) ^ near) * 4 + (step - array % 4 + 4) % 4
        piece = col * per_col + tile % per_col
        base = tile * slots + piece * width * 256

        def live(state):
            slot, _ = state
            return (slot < slots) & (ham[tile, slot] >= 0)

        def one_slot(state):
            slot, count = state
            key = ham[tile, slot]
            row = key // 8
            inner = key % 8
            for w in range(2):
                there = iterate[piece, inner * 2 + w]
                for v in range(2):
                    pairs[count] = base + slot + (inner * 2 + w) * 256 + (row * 2 + v) * 65536
                    count = count + (aim[row * 2 + v] == there).astype(jnp.int32)
            return slot + 1, count

        return lax.while_loop(live, one_slot, (jnp.int32(0), count))[1]

    pairs[pairs.shape[0] - 1] = lax.fori_loop(0, pieces, one_tile, jnp.int32(0))
    pairs[pairs.shape[0] - 2] = where[1]


def product_kernel(pairs, iterate, *rest):
    hams, (sent_on, sent_keep, kept_on, kept_keep, total, ham_buf, it_buf, ham_sem, it_sem) = rest[:8], rest[8:]
    size = ham_buf.shape[1]
    slots = hams[0].shape[0] // size
    count = pairs[pairs.shape[0] - 1]

    def start(at):
        code = pairs[at]
        ham_at = code % 256
        slot = at % WINDOW
        rows = pl.ds(pl.multiple_of((ham_at % slots) * size, size), size)
        for k, ham in enumerate(hams):

            @pl.when(ham_at // slots == k)
            def _():
                pltpu.make_async_copy(ham.at[rows], ham_buf.at[slot], ham_sem.at[slot]).start()

        pltpu.make_async_copy(iterate.at[(code // 256) % 256], it_buf.at[slot], it_sem.at[slot]).start()

    def first(at, carry):
        start(at)
        return carry

    lax.fori_loop(0, jnp.minimum(count, WINDOW), first, 0)

    def clear(at, carry):
        total[at] = jnp.zeros(total.shape[1:], total.dtype)
        return carry

    lax.fori_loop(0, total.shape[0], clear, 0, unroll=4)

    def multiply(at, carry):
        slot = at % WINDOW
        pltpu.make_async_copy(hams[0].at[pl.ds(0, size)], ham_buf.at[slot], ham_sem.at[slot]).wait()
        pltpu.make_async_copy(iterate.at[0], it_buf.at[slot], it_sem.at[slot]).wait()
        goal = pairs[at] // 65536
        total[goal] += jnp.dot(ham_buf[slot], it_buf[slot], preferred_element_type=jnp.float32)

        @pl.when(at + WINDOW < count)
        def _():
            start(at + WINDOW)

        return carry

    lax.fori_loop(0, count, multiply, 0)
    half = sent_on.shape[0]
    depth = pairs[pairs.shape[0] - 2]
    core = depth % 2
    high = depth // 2

    def finish(at, carry):
        away = (1 - high) * 2
        home = high * 2
        sent_on[at] = total[(away + 1 - core) * half + at].astype(sent_on.dtype)
        kept_on[at] = total[(away + core) * half + at].astype(kept_on.dtype)
        sent_keep[at] = total[(home + 1 - core) * half + at].astype(sent_keep.dtype)
        kept_keep[at] = total[(home + core) * half + at].astype(kept_keep.dtype)
        return carry

    lax.fori_loop(0, half, finish, 0, unroll=2)


def body(h_blocks, h_rows, h_cols, h_flags, x_blocks, x_cols, x_flags, previous):
    block = x_blocks.shape[-1]
    n_row, n_col, n_depth = lax.axis_size("row"), lax.axis_size("col"), lax.axis_size("depth")
    where = jnp.stack([lax.axis_index("col"), lax.axis_index("depth")]).astype(jnp.int32)
    iterate = lax.all_gather(x_blocks[0, 0, 0], "row", axis=0)
    iterate = iterate.reshape(-1, block, block)
    it_ints = jnp.concatenate([x_cols, x_flags], axis=2)
    slots = h_rows.shape[-1]
    ham_ints = jnp.concatenate([ints.reshape(-1, slots) for ints in (h_rows, h_cols, h_flags)], axis=0)
    ham_ints = ham_ints.astype(jnp.bfloat16)
    ham_ints = jnp.pad(ham_ints, ((0, 16 - ham_ints.shape[0]), (0, block - slots)))
    mine = jnp.concatenate([h_blocks.reshape(-1, block), ham_ints], axis=0)

    def send(source, flip, step):
        route = [(c, ((c // 4) ^ flip) * 4 + (c % 4 + step) % 4) for c in range(n_col)]
        return lax.ppermute(source, "col", route)

    hams = [mine] + [None] * (n_col - 1)
    for flip, step in ((1, 0), (1, 2), (0, 2), (1, 1), (1, 3)):
        hams[flip * 4 + step] = send(mine, flip, step)
    hams[4], it_ints = lax.optimization_barrier((hams[4], it_ints))
    aim_ints = lax.all_gather(it_ints, "depth", axis=1, tiled=True)
    it_ints = lax.all_gather(it_ints, "row", axis=0, tiled=True)
    late, aim_ints, it_ints = lax.optimization_barrier((mine, aim_ints, it_ints))
    for flip, step in ((0, 1), (0, 3)):
        hams[flip * 4 + step] = send(late, flip, step)
    hams = [pltpu.with_memory_space_constraint(ham, pltpu.HBM) for ham in hams]
    it_keys = jnp.where(it_ints[:, 0, 1] > 0, it_ints[:, 0, 0], -1).reshape(n_row, -1)
    aim_keys = jnp.where(aim_ints[0, :, 1] > 0, aim_ints[0, :, 0], -2).reshape(-1)
    smem = pl.BlockSpec(memory_space=pltpu.SMEM)
    anywhere = pl.BlockSpec(memory_space=pl.ANY)
    vmem = pl.BlockSpec(memory_space=pltpu.VMEM)
    ham_keys = pl.pallas_call(
        key_kernel,
        out_shape=jax.ShapeDtypeStruct((n_row, block), jnp.int32),
        in_specs=[anywhere] * n_col,
        out_specs=vmem,
        scratch_shapes=[pltpu.VMEM((n_col, 16, block), jnp.bfloat16), pltpu.SemaphoreType.DMA((n_col,))],
        name="keys",
    )(*hams)
    pairs = pl.pallas_call(
        pair_kernel,
        out_shape=jax.ShapeDtypeStruct((512,), jnp.int32),
        in_specs=[smem] * 4,
        out_specs=smem,
        name="pairs",
    )(where, ham_keys, it_keys, aim_keys)
    results = x_cols.shape[3] * x_cols.shape[4]
    part = jax.ShapeDtypeStruct((results, block, block), jnp.bfloat16)
    sent_on, sent_keep, kept_on, kept_keep = pl.pallas_call(
        product_kernel,
        out_shape=(part,) * 4,
        in_specs=[smem] + [anywhere] * 9,
        out_specs=(vmem,) * 4,
        scratch_shapes=[
            pltpu.VMEM((n_depth * results, block, block), jnp.float32),
            pltpu.VMEM((WINDOW, block, block), jnp.bfloat16),
            pltpu.VMEM((WINDOW, block, block), jnp.bfloat16),
            pltpu.SemaphoreType.DMA((WINDOW,)),
            pltpu.SemaphoreType.DMA((WINDOW,)),
        ],
        compiler_params=pltpu.CompilerParams(vmem_limit_bytes=24 << 20),
        name="products",
    )(*[pltpu.with_memory_space_constraint(x, pltpu.HBM) for x in (pairs, iterate)], *hams)
    to_core = [(d, d ^ 1) for d in range(n_depth)]
    near_on = lax.ppermute(sent_on, "depth", to_core)
    onward = (kept_on.astype(jnp.float32) + near_on.astype(jnp.float32)).astype(jnp.bfloat16)
    onward, sent_keep = lax.optimization_barrier((onward, sent_keep))
    far = lax.ppermute(onward, "depth", [(d, d ^ 2) for d in range(n_depth)])
    near_keep = lax.ppermute(sent_keep, "depth", to_core)
    prior = previous.reshape(results, block, block).astype(jnp.float32)
    live = x_flags.reshape(results, 1, 1).astype(jnp.float32)
    summed = kept_keep.astype(jnp.float32) + near_keep.astype(jnp.float32)
    base = lax.optimization_barrier(2.0 * summed - prior)
    result = (base + 2.0 * far.astype(jnp.float32)) * live
    return result.astype(jnp.bfloat16).reshape(previous.shape)


def solution(mesh):
    placed = (
        P("row", "col", "depth", None, None, None),
        P("row", "col", "depth", None),
        P("row", "col", "depth", None),
        P("row", "col", "depth", None),
        P("row", "depth", "col", None, None, None, None),
        P("row", "depth", "col", None, None),
        P("row", "depth", "col", None, None),
        P("row", "depth", "col", None, None, None, None),
    )
    return jax.shard_map(
        body,
        mesh=mesh,
        in_specs=placed,
        out_specs=P("row", "depth", "col", None, None, None, None),
        check_vma=False,
    )
```

```python
import jax
import jax.numpy as jnp
from jax import lax
from jax.experimental import pallas as pl
from jax.experimental.pallas import tpu as pltpu
from jax.sharding import PartitionSpec as P

WINDOW = 16


def key_kernel(*refs):
    hams, (keys, slab, sem) = refs[:8], refs[8:]
    tail = slab.shape[1]
    copies = [
        pltpu.make_async_copy(ham.at[pl.ds(ham.shape[0] - tail, tail)], slab.at[k], sem.at[k])
        for k, ham in enumerate(hams)
    ]
    for copy in copies:
        copy.start()
    for k, copy in enumerate(copies):
        copy.wait()
        held = slab[k].astype(jnp.float32)
        for t in range(2):
            row, col, flag = (held[3 * t + i : 3 * t + i + 1] for i in range(3))
            place = jnp.where(flag > 0, row * 8 + col, -1.0)
            keys[2 * k + t : 2 * k + t + 1] = place.astype(jnp.int32)


def pair_kernel(where, ham, iterate, aim, pairs):
    pieces = ham.shape[0]
    slots = 12
    per_col = pieces // 8
    width = iterate.shape[1]
    near = where[0] // 4
    step = where[0] % 4

    def one_tile(tile, count):
        array = tile // per_col
        col = ((array // 4) ^ near) * 4 + (step - array % 4 + 4) % 4
        piece = col * per_col + tile % per_col
        base = tile * slots + piece * width * 256

        def live(state):
            slot, _ = state
            return (slot < slots) & (ham[tile, slot] >= 0)

        def one_slot(state):
            slot, count = state
            key = ham[tile, slot]
            row = key // 8
            inner = key % 8
            for w in range(2):
                there = iterate[piece, inner * 2 + w]
                for v in range(2):
                    pairs[count] = base + slot + (inner * 2 + w) * 256 + (row * 2 + v) * 65536
                    count = count + (aim[row * 2 + v] == there).astype(jnp.int32)
            return slot + 1, count

        return lax.while_loop(live, one_slot, (jnp.int32(0), count))[1]

    pairs[pairs.shape[0] - 1] = lax.fori_loop(0, pieces, one_tile, jnp.int32(0))
    pairs[pairs.shape[0] - 2] = where[1]


def product_kernel(pairs, iterate, *rest):
    hams, (sent, kept, total, ham_buf, it_buf, ham_sem, it_sem) = rest[:8], rest[8:]
    size = ham_buf.shape[1]
    slots = hams[0].shape[0] // size
    count = pairs[pairs.shape[0] - 1]

    def start(at):
        code = pairs[at]
        ham_at = code % 256
        slot = at % WINDOW
        rows = pl.ds(pl.multiple_of((ham_at % slots) * size, size), size)
        for k, ham in enumerate(hams):

            @pl.when(ham_at // slots == k)
            def _():
                pltpu.make_async_copy(ham.at[rows], ham_buf.at[slot], ham_sem.at[slot]).start()

        pltpu.make_async_copy(iterate.at[(code // 256) % 256], it_buf.at[slot], it_sem.at[slot]).start()

    def first(at, carry):
        start(at)
        return carry

    lax.fori_loop(0, jnp.minimum(count, WINDOW), first, 0)

    def clear(at, carry):
        total[at] = jnp.zeros(total.shape[1:], total.dtype)
        return carry

    lax.fori_loop(0, total.shape[0], clear, 0, unroll=4)

    def multiply(at, carry):
        slot = at % WINDOW
        pltpu.make_async_copy(hams[0].at[pl.ds(0, size)], ham_buf.at[slot], ham_sem.at[slot]).wait()
        pltpu.make_async_copy(iterate.at[0], it_buf.at[slot], it_sem.at[slot]).wait()
        goal = pairs[at] // 65536
        total[goal] += jnp.dot(ham_buf[slot], it_buf[slot], preferred_element_type=jnp.float32)

        @pl.when(at + WINDOW < count)
        def _():
            start(at + WINDOW)

        return carry

    lax.fori_loop(0, count, multiply, 0)
    half = sent.shape[1]
    depth = pairs[pairs.shape[0] - 2]
    core = depth % 2
    high = depth // 2

    def finish(at, carry):
        for part, far in enumerate((1 - high, high)):
            sent[part, at] = total[(far * 2 + 1 - core) * half + at].astype(sent.dtype)
            kept[part, at] = total[(far * 2 + core) * half + at].astype(kept.dtype)
        return carry

    lax.fori_loop(0, half, finish, 0, unroll=2)


def body(h_blocks, h_rows, h_cols, h_flags, x_blocks, x_cols, x_flags, previous):
    block = x_blocks.shape[-1]
    n_row, n_col, n_depth = lax.axis_size("row"), lax.axis_size("col"), lax.axis_size("depth")
    where = jnp.stack([lax.axis_index("col"), lax.axis_index("depth")]).astype(jnp.int32)
    iterate = lax.all_gather(x_blocks[0, 0, 0], "row", axis=0)
    iterate = iterate.reshape(-1, block, block)
    it_ints = jnp.concatenate([x_cols, x_flags], axis=2)
    aim_ints = lax.all_gather(it_ints, "depth", axis=1, tiled=True)
    slots = h_rows.shape[-1]
    ham_ints = jnp.concatenate([h_rows, h_cols, h_flags], axis=2).reshape(-1, slots)
    ham_ints = ham_ints.astype(jnp.bfloat16)
    ham_ints = jnp.pad(ham_ints, ((0, 16 - ham_ints.shape[0]), (0, block - slots)))
    mine = jnp.concatenate([h_blocks.reshape(-1, block), ham_ints], axis=0)
    mine, aim_ints = lax.optimization_barrier((mine, aim_ints))

    def send(source, flip, step):
        route = [(c, ((c // 4) ^ flip) * 4 + (c % 4 + step) % 4) for c in range(n_col)]
        return lax.ppermute(source, "col", route)

    hams = [mine] + [None] * (n_col - 1)
    for flip, step in ((1, 0), (1, 2), (0, 2), (1, 1), (1, 3)):
        hams[flip * 4 + step] = send(mine, flip, step)
    hams[4], it_ints = lax.optimization_barrier((hams[4], it_ints))
    it_ints = lax.all_gather(it_ints, "row", axis=0, tiled=True)
    late, it_ints = lax.optimization_barrier((mine, it_ints))
    for flip, step in ((0, 1), (0, 3)):
        hams[flip * 4 + step] = send(late, flip, step)
    hams = [pltpu.with_memory_space_constraint(ham, pltpu.HBM) for ham in hams]
    it_keys = jnp.where(it_ints[:, 0, 1] > 0, it_ints[:, 0, 0], -1).reshape(n_row, -1)
    aim_keys = jnp.where(aim_ints[0, :, 1] > 0, aim_ints[0, :, 0], -2).reshape(-1)
    smem = pl.BlockSpec(memory_space=pltpu.SMEM)
    anywhere = pl.BlockSpec(memory_space=pl.ANY)
    vmem = pl.BlockSpec(memory_space=pltpu.VMEM)
    ham_keys = pl.pallas_call(
        key_kernel,
        out_shape=jax.ShapeDtypeStruct((n_row, block), jnp.int32),
        in_specs=[anywhere] * n_col,
        out_specs=vmem,
        scratch_shapes=[pltpu.VMEM((n_col, 16, block), jnp.bfloat16), pltpu.SemaphoreType.DMA((n_col,))],
        name="keys",
    )(*hams)
    pairs = pl.pallas_call(
        pair_kernel,
        out_shape=jax.ShapeDtypeStruct((512,), jnp.int32),
        in_specs=[smem] * 4,
        out_specs=smem,
        name="pairs",
    )(where, ham_keys, it_keys, aim_keys)
    results = x_cols.shape[3] * x_cols.shape[4]
    halves = jax.ShapeDtypeStruct((2, results, block, block), jnp.bfloat16)
    sent, kept = pl.pallas_call(
        product_kernel,
        out_shape=(halves,) * 2,
        in_specs=[smem] + [anywhere] * 9,
        out_specs=(vmem,) * 2,
        scratch_shapes=[
            pltpu.VMEM((n_depth * results, block, block), jnp.float32),
            pltpu.VMEM((WINDOW, block, block), jnp.bfloat16),
            pltpu.VMEM((WINDOW, block, block), jnp.bfloat16),
            pltpu.SemaphoreType.DMA((WINDOW,)),
            pltpu.SemaphoreType.DMA((WINDOW,)),
        ],
        compiler_params=pltpu.CompilerParams(vmem_limit_bytes=24 << 20),
        name="products",
    )(*[pltpu.with_memory_space_constraint(x, pltpu.HBM) for x in (pairs, iterate)], *hams)
    near = lax.ppermute(sent, "depth", [(d, d ^ 1) for d in range(n_depth)])
    onward = (kept[0].astype(jnp.float32) + near[0].astype(jnp.float32)).astype(jnp.bfloat16)
    far = lax.ppermute(onward, "depth", [(d, d ^ 2) for d in range(n_depth)])
    prior = previous.reshape(results, block, block).astype(jnp.float32)
    live = x_flags.reshape(results, 1, 1).astype(jnp.float32)
    base = 2.0 * (kept[1].astype(jnp.float32) + near[1].astype(jnp.float32)) - prior
    base = lax.optimization_barrier(base)
    result = (base + 2.0 * far.astype(jnp.float32)) * live
    return result.astype(jnp.bfloat16).reshape(previous.shape)


def solution(mesh):
    placed = (
        P("row", "col", "depth", None, None, None),
        P("row", "col", "depth", None),
        P("row", "col", "depth", None),
        P("row", "col", "depth", None),
        P("row", "depth", "col", None, None, None, None),
        P("row", "depth", "col", None, None),
        P("row", "depth", "col", None, None),
        P("row", "depth", "col", None, None, None, None),
    )
    return jax.shard_map(
        body,
        mesh=mesh,
        in_specs=placed,
        out_specs=P("row", "depth", "col", None, None, None, None),
        check_vma=False,
    )
```

```python
import jax
import jax.numpy as jnp
from jax import lax
from jax.experimental import pallas as pl
from jax.experimental.pallas import tpu as pltpu
from jax.sharding import PartitionSpec as P

WINDOW = 16
SLOTS = 12


def by_offset(lines):
    both, ahead, back, across, across_beside = lines
    return [both.at[0], ahead.at[0], across, back.at[0], both.at[1], ahead.at[1], across_beside, back.at[1]]


def key_kernel(*refs):
    lines, shards, (ham_keys, it_keys, ham_slab, it_slab, sem) = refs[:5], refs[5:-5], refs[-5:]
    tail = ham_slab.shape[1]
    n_ham = ham_slab.shape[0]
    shards = by_offset(lines) + list(shards)
    copies = []
    for k, shard in enumerate(shards):
        slab = ham_slab.at[k] if k < n_ham else it_slab.at[k - n_ham]
        copies.append(pltpu.make_async_copy(shard.at[pl.ds(shard.shape[0] - tail, tail)], slab, sem.at[k]))
    for copy in copies:
        copy.start()
    for k, copy in enumerate(copies):
        copy.wait()
        if k < n_ham:
            held = ham_slab[k].astype(jnp.float32)
            for t in range(2):
                row, col, flag = (held[3 * t + i : 3 * t + i + 1] for i in range(3))
                place = jnp.where(flag > 0, row * 8 + col, -1.0)
                ham_keys[2 * k + t : 2 * k + t + 1] = place.astype(jnp.int32)
        else:
            held = it_slab[k - n_ham].astype(jnp.float32)
            place = jnp.where(held[1:2] > 0, held[0:1], -1.0)
            it_keys[k - n_ham : k - n_ham + 1] = place.astype(jnp.int32)


def list_tile(tile, hop, count, ham, own_keys, aim, pairs, slots):
    base = tile * slots + hop * 16 * 256

    def live(state):
        slot, _ = state
        return (slot < slots) & (ham[tile, slot] >= 0)

    def one_slot(state):
        slot, count = state
        key = ham[tile, slot]
        row = key // 8
        inner = key % 8
        for w in range(2):
            there = own_keys(inner * 2 + w)
            for v in range(2):
                pairs[count] = base + slot + (inner * 2 + w) * 256 + (row * 2 + v) * 65536
                count = count + (aim[row * 2 + v] == there).astype(jnp.int32)
        return slot + 1, count

    return lax.while_loop(live, one_slot, (jnp.int32(0), count))[1]


def pair_kernel(where, ham, iterate, aim, pairs):
    tiles = ham.shape[0]
    pieces = iterate.shape[0] + 1
    last = pieces // 2
    near = where[0] // 4
    step = where[0] % 4

    def one_tile(tile, count):
        array = tile // 2
        col = ((array // 4) ^ near) * 4 + (step - array % 4 + 4) % 4
        piece = col * 2 + tile % 2
        hop = (where[2] - piece + pieces) % pieces
        at = jnp.minimum(jnp.where(hop > last, hop - 1, hop), pieces - 2)
        keys = lambda spot: iterate[at, spot]
        listed = list_tile(tile, hop, count, ham, keys, aim, pairs, SLOTS)
        return jnp.where(hop == last, count, listed)

    end = pairs.shape[0]
    pairs[end - 1] = lax.fori_loop(0, tiles, one_tile, jnp.int32(0))
    pairs[end - 2] = where[1]
    piece = (where[2] + last) % pieces
    col = piece // 2
    array = ((col // 4) ^ near) * 4 + (step - col % 4 + 4) % 4
    pairs[end - 3] = array * 2 + piece % 2


def product_kernel(pairs, ham_keys, aim, *rest):
    lines, shards, rest = rest[:5], rest[5:22], rest[22:]
    hams = by_offset(lines)
    sent, kept, total, ham_buf, it_buf, slab, key_row, late_keys, late_pairs, ham_sem, it_sem, late_sem = rest
    size = ham_buf.shape[1]
    end = pairs.shape[0]
    count = pairs[end - 1]
    last = 8
    tail = slab.shape[0]
    slab_copy = pltpu.make_async_copy(shards[last].at[pl.ds(shards[last].shape[0] - tail, tail)], slab, late_sem.at[0])
    slab_copy.start()

    def start(codes, at):
        code = codes[at]
        ham_at = code % 256
        spot = (code // 256) % 16
        hop = (code // 4096) % 16
        slot = at % WINDOW
        rows = pl.ds(pl.multiple_of((ham_at % (2 * SLOTS)) * size, size), size)
        for k, ham in enumerate(hams):

            @pl.when(ham_at // (2 * SLOTS) == k)
            def _():
                pltpu.make_async_copy(ham.at[rows], ham_buf.at[slot], ham_sem.at[slot]).start()

        source = jnp.where((hop == last) & (spot < 8), 16, hop)
        rows = pl.ds(pl.multiple_of(jnp.where(hop == last, spot % 8, spot) * size, size), size)
        for k, shard in enumerate(shards):

            @pl.when(source == k)
            def _():
                pltpu.make_async_copy(shard.at[rows], it_buf.at[slot], it_sem.at[slot]).start()

    def prime(codes, count):
        def first(at, carry):
            start(codes, at)
            return carry

        lax.fori_loop(0, jnp.minimum(count, WINDOW), first, 0)

    def drain(codes, count):
        def multiply(at, carry):
            slot = at % WINDOW
            pltpu.make_async_copy(hams[0].at[pl.ds(0, size)], ham_buf.at[slot], ham_sem.at[slot]).wait()
            pltpu.make_async_copy(shards[0].at[pl.ds(0, size)], it_buf.at[slot], it_sem.at[slot]).wait()
            goal = codes[at] // 65536
            total[goal] += jnp.dot(ham_buf[slot], it_buf[slot], preferred_element_type=jnp.float32)

            @pl.when(at + WINDOW < count)
            def _():
                start(codes, at + WINDOW)

            return carry

        lax.fori_loop(0, count, multiply, 0)

    prime(pairs, count)

    def clear(at, carry):
        total[at] = jnp.zeros(total.shape[1:], total.dtype)
        return carry

    lax.fori_loop(0, total.shape[0], clear, 0, unroll=4)
    slab_copy.wait()
    held = slab[...].astype(jnp.float32)
    key_row[...] = jnp.where(held[1:2] > 0, held[0:1], -1.0).astype(jnp.int32)
    key_copy = pltpu.make_async_copy(key_row, late_keys, late_sem.at[1])
    key_copy.start()
    drain(pairs, count)
    key_copy.wait()
    late = list_tile(pairs[end - 3], last, jnp.int32(0), ham_keys, lambda spot: late_keys[0, spot], aim, late_pairs, SLOTS)
    prime(late_pairs, late)
    drain(late_pairs, late)
    half = sent.shape[1]
    depth = pairs[end - 2]
    core = depth % 2
    high = depth // 2

    def finish(at, carry):
        for part, far in enumerate((1 - high, high)):
            sent[part, at] = total[(far * 2 + 1 - core) * half + at].astype(sent.dtype)
            kept[part, at] = total[(far * 2 + core) * half + at].astype(kept.dtype)
        return carry

    lax.fori_loop(0, half, finish, 0, unroll=2)


def with_tail(blocks, ints):
    width = blocks.shape[-1]
    ints = ints.astype(blocks.dtype)
    ints = jnp.pad(ints, ((0, 16 - ints.shape[0]), (0, width - ints.shape[1])))
    return jnp.concatenate([blocks.reshape(-1, width), ints], axis=0)


def body(h_blocks, h_rows, h_cols, h_flags, x_blocks, x_cols, x_flags, previous):
    block = x_blocks.shape[-1]
    n_row, n_col, n_depth = lax.axis_size("row"), lax.axis_size("col"), lax.axis_size("depth")
    results = x_cols.shape[3] * x_cols.shape[4]
    where = jnp.stack([lax.axis_index("col"), lax.axis_index("depth"), lax.axis_index("row")]).astype(jnp.int32)
    x_ints = jnp.concatenate([x_cols.reshape(1, -1), x_flags.reshape(1, -1)], axis=0)
    own = with_tail(x_blocks, x_ints)
    h_ints = jnp.concatenate([h_rows, h_cols, h_flags], axis=2).reshape(-1, SLOTS)
    mine = with_tail(h_blocks, h_ints)

    up = [(i, (i + 1) % n_row) for i in range(n_row)]
    down = [(i, (i - 1) % n_row) for i in range(n_row)]
    last = n_row // 2
    cut = (results // 2) * block
    shards = [own] + [None] * n_row
    shards[1] = lax.ppermute(own, "row", up)
    shards[n_row - 1] = lax.ppermute(own, "row", down)
    beside = lax.ppermute(mine, "col", [(c, c ^ 4) for c in range(n_col)])
    pattern = jnp.concatenate([x_cols, x_flags], axis=2)
    beside, pattern = lax.optimization_barrier((beside, pattern))
    aim_ints = lax.all_gather(pattern, "depth", axis=1, tiled=True)
    both = jnp.stack([mine, beside])
    ahead = [(c, (c // 4) * 4 + (c + 1) % 4) for c in range(n_col)]
    back = [(c, (c // 4) * 4 + (c + 3) % 4) for c in range(n_col)]
    line_ahead = lax.ppermute(both, "col", ahead)
    line_back = lax.ppermute(both, "col", back)
    across = lax.ppermute(line_ahead[0], "col", ahead)
    across_beside = lax.ppermute(line_back[1], "col", back)
    lines = [both, line_ahead, line_back, across, across_beside]
    for hop in range(2, last):
        if hop == 5:
            shards[hop - 1], aim_ints = lax.optimization_barrier((shards[hop - 1], aim_ints))
        shards[hop] = lax.ppermute(shards[hop - 1], "row", up)
        shards[n_row - hop] = lax.ppermute(shards[n_row - hop + 1], "row", down)
    shards[last - 1], shards[last + 1], lines[3], lines[4] = lax.optimization_barrier(
        (shards[last - 1], shards[last + 1], lines[3], lines[4])
    )
    shards[last] = lax.ppermute(shards[last - 1][cut:], "row", up)
    shards[n_row] = lax.ppermute(shards[last + 1][:cut], "row", down)
    lines, shards = ([pltpu.with_memory_space_constraint(x, pltpu.HBM) for x in xs] for xs in (lines, shards))

    aim_keys = jnp.where(aim_ints[0, :, 1] > 0, aim_ints[0, :, 0], -2).reshape(-1)
    smem = pl.BlockSpec(memory_space=pltpu.SMEM)
    anywhere = pl.BlockSpec(memory_space=pl.ANY)
    vmem = pl.BlockSpec(memory_space=pltpu.VMEM)
    early = shards[:last] + shards[last + 1 : n_row]
    ham_keys, it_keys = pl.pallas_call(
        key_kernel,
        out_shape=(
            jax.ShapeDtypeStruct((2 * n_col, block), jnp.int32),
            jax.ShapeDtypeStruct((len(early), block), jnp.int32),
        ),
        in_specs=[anywhere] * (len(lines) + len(early)),
        out_specs=(vmem, vmem),
        scratch_shapes=[
            pltpu.VMEM((n_col, 16, block), jnp.bfloat16),
            pltpu.VMEM((len(early), 16, block), jnp.bfloat16),
            pltpu.SemaphoreType.DMA((n_col + len(early),)),
        ],
        name="keys",
    )(*lines, *early)
    pairs = pl.pallas_call(
        pair_kernel,
        out_shape=jax.ShapeDtypeStruct((512,), jnp.int32),
        in_specs=[smem] * 4,
        out_specs=smem,
        name="pairs",
    )(where, ham_keys, it_keys, aim_keys)
    halves = jax.ShapeDtypeStruct((2, results, block, block), jnp.bfloat16)
    sent, kept = pl.pallas_call(
        product_kernel,
        out_shape=(halves,) * 2,
        in_specs=[smem] * 3 + [anywhere] * (len(lines) + n_row + 1),
        out_specs=(vmem,) * 2,
        scratch_shapes=[
            pltpu.VMEM((n_depth * results, block, block), jnp.float32),
            pltpu.VMEM((WINDOW, block, block), jnp.bfloat16),
            pltpu.VMEM((WINDOW, block, block), jnp.bfloat16),
            pltpu.VMEM((16, block), jnp.bfloat16),
            pltpu.VMEM((1, block), jnp.int32),
            pltpu.SMEM((1, block), jnp.int32),
            pltpu.SMEM((64,), jnp.int32),
            pltpu.SemaphoreType.DMA((WINDOW,)),
            pltpu.SemaphoreType.DMA((WINDOW,)),
            pltpu.SemaphoreType.DMA((2,)),
        ],
        compiler_params=pltpu.CompilerParams(vmem_limit_bytes=24 << 20),
        name="products",
    )(*[pltpu.with_memory_space_constraint(x, pltpu.HBM) for x in (pairs, ham_keys, aim_keys)], *lines, *shards)
    near = lax.ppermute(sent, "depth", [(d, d ^ 1) for d in range(n_depth)])
    onward = (kept[0].astype(jnp.float32) + near[0].astype(jnp.float32)).astype(jnp.bfloat16)
    far = lax.ppermute(onward, "depth", [(d, d ^ 2) for d in range(n_depth)])
    prior = previous.reshape(results, block, block).astype(jnp.float32)
    live = x_flags.reshape(results, 1, 1).astype(jnp.float32)
    base = 2.0 * (kept[1].astype(jnp.float32) + near[1].astype(jnp.float32)) - prior
    base = lax.optimization_barrier(base)
    result = (base + 2.0 * far.astype(jnp.float32)) * live
    return result.astype(jnp.bfloat16).reshape(previous.shape)


def solution(mesh):
    placed = (
        P("row", "col", "depth", None, None, None),
        P("row", "col", "depth", None),
        P("row", "col", "depth", None),
        P("row", "col", "depth", None),
        P("row", "depth", "col", None, None, None, None),
        P("row", "depth", "col", None, None),
        P("row", "depth", "col", None, None),
        P("row", "depth", "col", None, None, None, None),
    )
    return jax.shard_map(
        body,
        mesh=mesh,
        in_specs=placed,
        out_specs=P("row", "depth", "col", None, None, None, None),
        check_vma=False,
    )
```

```python
import jax
import jax.numpy as jnp
from jax import lax
from jax.experimental import pallas as pl
from jax.experimental.pallas import tpu as pltpu
from jax.sharding import PartitionSpec as P

WINDOW = 16


def key_kernel(*refs):
    hams, (keys, slab, sem) = refs[:8], refs[8:]
    tail = slab.shape[1]
    copies = [
        pltpu.make_async_copy(ham.at[pl.ds(ham.shape[0] - tail, tail)], slab.at[k], sem.at[k])
        for k, ham in enumerate(hams)
    ]
    for copy in copies:
        copy.start()
    for k, copy in enumerate(copies):
        copy.wait()
        held = slab[k].astype(jnp.float32)
        for t in range(2):
            row, col, flag = (held[3 * t + i : 3 * t + i + 1] for i in range(3))
            place = jnp.where(flag > 0, row * 8 + col, -1.0)
            keys[2 * k + t : 2 * k + t + 1] = place.astype(jnp.int32)


def pair_kernel(where, ham, iterate, aim, pairs, touched):
    def untouch(at, carry):
        touched[at] = 0
        return carry

    lax.fori_loop(0, aim.shape[0], untouch, 0)
    pieces = ham.shape[0]
    slots = 12
    per_col = pieces // 8
    width = iterate.shape[1]
    near = where[0] // 4
    step = where[0] % 4

    def one_tile(tile, count):
        array = tile // per_col
        col = ((array // 4) ^ near) * 4 + (step - array % 4 + 4) % 4
        piece = col * per_col + tile % per_col
        base = tile * slots + piece * width * 256

        def live(state):
            slot, _ = state
            return (slot < slots) & (ham[tile, slot] >= 0)

        def one_slot(state):
            slot, count = state
            key = ham[tile, slot]
            row = key // 8
            inner = key % 8
            for w in range(2):
                there = iterate[piece, inner * 2 + w]
                for v in range(2):
                    goal = row * 2 + v
                    match = (aim[goal] == there).astype(jnp.int32)
                    seen = touched[goal]
                    pairs[count] = base + slot + (inner * 2 + w) * 256 + (goal + 64 * seen) * 65536
                    touched[goal] = seen | match
                    count = count + match
            return slot + 1, count

        return lax.while_loop(live, one_slot, (jnp.int32(0), count))[1]

    pairs[pairs.shape[0] - 1] = lax.fori_loop(0, pieces, one_tile, jnp.int32(0))
    pairs[pairs.shape[0] - 2] = where[1]


def product_kernel(pairs, iterate, *rest):
    hams, (sent, kept, total, ham_buf, it_buf, ham_sem, it_sem) = rest[:8], rest[8:]
    size = ham_buf.shape[1]
    slots = hams[0].shape[0] // size
    count = pairs[pairs.shape[0] - 1]

    def start(at):
        code = pairs[at]
        ham_at = code % 256
        slot = at % WINDOW
        rows = pl.ds(pl.multiple_of((ham_at % slots) * size, size), size)
        for k, ham in enumerate(hams):

            @pl.when(ham_at // slots == k)
            def _():
                pltpu.make_async_copy(ham.at[rows], ham_buf.at[slot], ham_sem.at[slot]).start()

        pltpu.make_async_copy(iterate.at[(code // 256) % 256], it_buf.at[slot], it_sem.at[slot]).start()

    def first(at, carry):
        start(at)
        return carry

    lax.fori_loop(0, jnp.minimum(count, WINDOW), first, 0)

    half = sent.shape[1]
    depth = pairs[pairs.shape[0] - 2]
    core = depth % 2
    high = depth // 2

    def clear(at, carry):
        for part in range(2):
            sent[part, at] = jnp.zeros(sent.shape[2:], sent.dtype)
            kept[part, at] = jnp.zeros(kept.shape[2:], kept.dtype)
        return carry

    lax.fori_loop(0, half, clear, 0, unroll=4)

    def multiply(at, carry):
        slot = at % WINDOW
        pltpu.make_async_copy(hams[0].at[pl.ds(0, size)], ham_buf.at[slot], ham_sem.at[slot]).wait()
        pltpu.make_async_copy(iterate.at[0], it_buf.at[slot], it_sem.at[slot]).wait()
        goal = pairs[at] // 65536
        seen = goal >= 64
        goal = goal % 64
        product = jnp.dot(ham_buf[slot], it_buf[slot], preferred_element_type=jnp.float32)
        product = jnp.where(seen, total[goal], 0.0) + product
        total[goal] = product
        owner = goal // half
        part = (owner // 2 == high).astype(jnp.int32)

        @pl.when(owner % 2 == core)
        def _():
            kept[part, goal % half] = product.astype(kept.dtype)

        @pl.when(owner % 2 != core)
        def _():
            sent[part, goal % half] = product.astype(sent.dtype)

        @pl.when(at + WINDOW < count)
        def _():
            start(at + WINDOW)

        return carry

    lax.fori_loop(0, count, multiply, 0)


def body(h_blocks, h_rows, h_cols, h_flags, x_blocks, x_cols, x_flags, previous):
    block = x_blocks.shape[-1]
    n_row, n_col, n_depth = lax.axis_size("row"), lax.axis_size("col"), lax.axis_size("depth")
    where = jnp.stack([lax.axis_index("col"), lax.axis_index("depth")]).astype(jnp.int32)
    iterate = lax.all_gather(x_blocks[0, 0, 0], "row", axis=0)
    iterate = iterate.reshape(-1, block, block)
    it_ints = jnp.concatenate([x_cols, x_flags], axis=2)
    aim_ints = lax.all_gather(it_ints, "depth", axis=1, tiled=True)
    slots = h_rows.shape[-1]
    ham_ints = jnp.concatenate([h_rows, h_cols, h_flags], axis=2).reshape(-1, slots)
    ham_ints = ham_ints.astype(jnp.bfloat16)
    ham_ints = jnp.pad(ham_ints, ((0, 16 - ham_ints.shape[0]), (0, block - slots)))
    mine = jnp.concatenate([h_blocks.reshape(-1, block), ham_ints], axis=0)
    mine, aim_ints = lax.optimization_barrier((mine, aim_ints))

    def send(source, flip, step):
        route = [(c, ((c // 4) ^ flip) * 4 + (c % 4 + step) % 4) for c in range(n_col)]
        return lax.ppermute(source, "col", route)

    hams = [mine] + [None] * (n_col - 1)
    for flip, step in ((1, 0), (1, 2), (0, 2), (1, 1), (1, 3)):
        hams[flip * 4 + step] = send(mine, flip, step)
    hams[4], it_ints = lax.optimization_barrier((hams[4], it_ints))
    it_ints = lax.all_gather(it_ints, "row", axis=0, tiled=True)
    late, it_ints = lax.optimization_barrier((mine, it_ints))
    for flip, step in ((0, 1), (0, 3)):
        hams[flip * 4 + step] = send(late, flip, step)
    hams = [pltpu.with_memory_space_constraint(ham, pltpu.HBM) for ham in hams]
    it_keys = jnp.where(it_ints[:, 0, 1] > 0, it_ints[:, 0, 0], -1).reshape(n_row, -1)
    aim_keys = jnp.where(aim_ints[0, :, 1] > 0, aim_ints[0, :, 0], -2).reshape(-1)
    smem = pl.BlockSpec(memory_space=pltpu.SMEM)
    anywhere = pl.BlockSpec(memory_space=pl.ANY)
    vmem = pl.BlockSpec(memory_space=pltpu.VMEM)
    ham_keys = pl.pallas_call(
        key_kernel,
        out_shape=jax.ShapeDtypeStruct((n_row, block), jnp.int32),
        in_specs=[anywhere] * n_col,
        out_specs=vmem,
        scratch_shapes=[pltpu.VMEM((n_col, 16, block), jnp.bfloat16), pltpu.SemaphoreType.DMA((n_col,))],
        name="keys",
    )(*hams)
    results = x_cols.shape[3] * x_cols.shape[4]
    halves = jax.ShapeDtypeStruct((2, results, block, block), jnp.bfloat16)
    pairs = pl.pallas_call(
        pair_kernel,
        out_shape=jax.ShapeDtypeStruct((512,), jnp.int32),
        in_specs=[smem] * 4,
        out_specs=smem,
        scratch_shapes=[pltpu.SMEM((n_depth * results,), jnp.int32)],
        name="pairs",
    )(where, ham_keys, it_keys, aim_keys)
    sent, kept = pl.pallas_call(
        product_kernel,
        out_shape=(halves,) * 2,
        in_specs=[smem] + [anywhere] * 9,
        out_specs=(vmem,) * 2,
        scratch_shapes=[
            pltpu.VMEM((n_depth * results, block, block), jnp.float32),
            pltpu.VMEM((WINDOW, block, block), jnp.bfloat16),
            pltpu.VMEM((WINDOW, block, block), jnp.bfloat16),
            pltpu.SemaphoreType.DMA((WINDOW,)),
            pltpu.SemaphoreType.DMA((WINDOW,)),
        ],
        compiler_params=pltpu.CompilerParams(vmem_limit_bytes=24 << 20),
        name="products",
    )(*[pltpu.with_memory_space_constraint(x, pltpu.HBM) for x in (pairs, iterate)], *hams)
    near = lax.ppermute(sent, "depth", [(d, d ^ 1) for d in range(n_depth)])
    onward = (kept[0].astype(jnp.float32) + near[0].astype(jnp.float32)).astype(jnp.bfloat16)
    far = lax.ppermute(onward, "depth", [(d, d ^ 2) for d in range(n_depth)])
    prior = previous.reshape(results, block, block).astype(jnp.float32)
    live = x_flags.reshape(results, 1, 1).astype(jnp.float32)
    base = 2.0 * (kept[1].astype(jnp.float32) + near[1].astype(jnp.float32)) - prior
    base = lax.optimization_barrier(base)
    result = (base + 2.0 * far.astype(jnp.float32)) * live
    return result.astype(jnp.bfloat16).reshape(previous.shape)


def solution(mesh):
    placed = (
        P("row", "col", "depth", None, None, None),
        P("row", "col", "depth", None),
        P("row", "col", "depth", None),
        P("row", "col", "depth", None),
        P("row", "depth", "col", None, None, None, None),
        P("row", "depth", "col", None, None),
        P("row", "depth", "col", None, None),
        P("row", "depth", "col", None, None, None, None),
    )
    return jax.shard_map(
        body,
        mesh=mesh,
        in_specs=placed,
        out_specs=P("row", "depth", "col", None, None, None, None),
        check_vma=False,
    )
```

```python
import jax
import jax.numpy as jnp
from jax import lax
from jax.experimental import pallas as pl
from jax.experimental.pallas import tpu as pltpu
from jax.sharding import PartitionSpec as P

WINDOW = 16


def key_kernel(*refs):
    hams, (keys, slab, sem) = refs[:8], refs[8:]
    tail = slab.shape[1]
    copies = [
        pltpu.make_async_copy(ham.at[pl.ds(ham.shape[0] - tail, tail)], slab.at[k], sem.at[k])
        for k, ham in enumerate(hams)
    ]
    for copy in copies:
        copy.start()
    for k, copy in enumerate(copies):
        copy.wait()
        held = slab[k].astype(jnp.float32)
        for t in range(2):
            row, col, flag = (held[3 * t + i : 3 * t + i + 1] for i in range(3))
            place = jnp.where(flag > 0, row * 8 + col, -1.0)
            keys[2 * k + t : 2 * k + t + 1] = place.astype(jnp.int32)


def pair_kernel(where, ham, iterate, aim, pairs, touched):
    def untouch(at, carry):
        touched[at] = 0
        return carry

    lax.fori_loop(0, aim.shape[0], untouch, 0)
    pieces = ham.shape[0]
    slots = 12
    per_col = pieces // 8
    width = iterate.shape[1]
    near = where[0] // 4
    step = where[0] % 4

    def one_tile(tile, count):
        array = tile // per_col
        col = ((array // 4) ^ near) * 4 + (step - array % 4 + 4) % 4
        piece = col * per_col + tile % per_col
        base = tile * slots + piece * width * 256

        def live(state):
            slot, _ = state
            return (slot < slots) & (ham[tile, slot] >= 0)

        def one_slot(state):
            slot, count = state
            key = ham[tile, slot]
            row = key // 8
            inner = key % 8
            for w in range(2):
                there = iterate[piece, inner * 2 + w]
                for v in range(2):
                    goal = row * 2 + v
                    match = (aim[goal] == there).astype(jnp.int32)
                    seen = touched[goal]
                    pairs[count] = base + slot + (inner * 2 + w) * 256 + (goal + 64 * seen) * 65536
                    touched[goal] = seen | match
                    count = count + match
            return slot + 1, count

        return lax.while_loop(live, one_slot, (jnp.int32(0), count))[1]

    pairs[pairs.shape[0] - 1] = lax.fori_loop(0, pieces, one_tile, jnp.int32(0))
    pairs[pairs.shape[0] - 2] = where[1]


def product_kernel(pairs, iterate, *rest):
    hams, (sent, kept, total, ham_buf, it_buf, ham_sem, it_sem) = rest[:8], rest[8:]
    size = ham_buf.shape[1]
    slots = hams[0].shape[0] // size
    count = pairs[pairs.shape[0] - 1]

    def start(at):
        code = pairs[at]
        ham_at = code % 256
        slot = at % WINDOW
        rows = pl.ds(pl.multiple_of((ham_at % slots) * size, size), size)
        for k, ham in enumerate(hams):

            @pl.when(ham_at // slots == k)
            def _():
                pltpu.make_async_copy(ham.at[rows], ham_buf.at[slot], ham_sem.at[slot]).start()

        pltpu.make_async_copy(iterate.at[(code // 256) % 256], it_buf.at[slot], it_sem.at[slot]).start()

    def first(at, carry):
        start(at)
        return carry

    lax.fori_loop(0, jnp.minimum(count, WINDOW), first, 0)

    half = sent.shape[1]
    depth = pairs[pairs.shape[0] - 2]
    core = depth % 2
    high = depth // 2

    def clear(at, carry):
        for part in range(2):
            sent[part, at] = jnp.zeros(sent.shape[2:], sent.dtype)
            kept[part, at] = jnp.zeros(kept.shape[2:], kept.dtype)
        return carry

    lax.fori_loop(0, half, clear, 0, unroll=4)

    def multiply(at, carry):
        slot = at % WINDOW
        pltpu.make_async_copy(hams[0].at[pl.ds(0, size)], ham_buf.at[slot], ham_sem.at[slot]).wait()
        pltpu.make_async_copy(iterate.at[0], it_buf.at[slot], it_sem.at[slot]).wait()
        goal = pairs[at] // 65536
        seen = goal >= 64
        goal = goal % 64
        product = jnp.dot(ham_buf[slot], it_buf[slot], preferred_element_type=jnp.float32)
        product = jnp.where(seen, total[goal], 0.0) + product
        total[goal] = product
        owner = goal // half
        part = (owner // 2 == high).astype(jnp.int32)

        @pl.when(owner % 2 == core)
        def _():
            kept[part, goal % half] = product.astype(kept.dtype)

        @pl.when(owner % 2 != core)
        def _():
            sent[part, goal % half] = product.astype(sent.dtype)

        @pl.when(at + WINDOW < count)
        def _():
            start(at + WINDOW)

        return carry

    lax.fori_loop(0, count, multiply, 0)


def body(h_blocks, h_rows, h_cols, h_flags, x_blocks, x_cols, x_flags, previous):
    block = x_blocks.shape[-1]
    n_row, n_col, n_depth = lax.axis_size("row"), lax.axis_size("col"), lax.axis_size("depth")
    where = jnp.stack([lax.axis_index("col"), lax.axis_index("depth")]).astype(jnp.int32)
    iterate = lax.all_gather(x_blocks[0, 0, 0], "row", axis=0)
    iterate = iterate.reshape(-1, block, block)
    it_ints = jnp.concatenate([x_cols, x_flags], axis=2)
    aim_ints = lax.all_gather(it_ints, "depth", axis=1, tiled=True)
    slots = h_rows.shape[-1]
    ham_ints = jnp.concatenate([h_rows, h_cols, h_flags], axis=2).reshape(-1, slots)
    ham_ints = ham_ints.astype(jnp.bfloat16)
    ham_ints = jnp.pad(ham_ints, ((0, 16 - ham_ints.shape[0]), (0, block - slots)))
    mine = jnp.concatenate([h_blocks.reshape(-1, block), ham_ints], axis=0)

    def send(source, flip, step):
        route = [(c, ((c // 4) ^ flip) * 4 + (c % 4 + step) % 4) for c in range(n_col)]
        return lax.ppermute(source, "col", route)

    hams = [mine] + [None] * (n_col - 1)
    for flip, step in ((0, 1), (0, 3)):
        hams[flip * 4 + step] = send(mine, flip, step)
    crossing, aim_ints = lax.optimization_barrier((mine, aim_ints))
    for flip, step in ((1, 0), (1, 2), (1, 1)):
        hams[flip * 4 + step] = send(crossing, flip, step)
    hams[1], crossing = lax.optimization_barrier((hams[1], crossing))
    hams[7] = send(crossing, 1, 3)
    hams[3], crossing, it_ints = lax.optimization_barrier((hams[3], crossing, it_ints))
    hams[2] = send(crossing, 0, 2)
    it_ints = lax.all_gather(it_ints, "row", axis=0, tiled=True)
    hams = [pltpu.with_memory_space_constraint(ham, pltpu.HBM) for ham in hams]
    it_keys = jnp.where(it_ints[:, 0, 1] > 0, it_ints[:, 0, 0], -1).reshape(n_row, -1)
    aim_keys = jnp.where(aim_ints[0, :, 1] > 0, aim_ints[0, :, 0], -2).reshape(-1)
    smem = pl.BlockSpec(memory_space=pltpu.SMEM)
    anywhere = pl.BlockSpec(memory_space=pl.ANY)
    vmem = pl.BlockSpec(memory_space=pltpu.VMEM)
    ham_keys = pl.pallas_call(
        key_kernel,
        out_shape=jax.ShapeDtypeStruct((n_row, block), jnp.int32),
        in_specs=[anywhere] * n_col,
        out_specs=vmem,
        scratch_shapes=[pltpu.VMEM((n_col, 16, block), jnp.bfloat16), pltpu.SemaphoreType.DMA((n_col,))],
        name="keys",
    )(*hams)
    results = x_cols.shape[3] * x_cols.shape[4]
    halves = jax.ShapeDtypeStruct((2, results, block, block), jnp.bfloat16)
    pairs = pl.pallas_call(
        pair_kernel,
        out_shape=jax.ShapeDtypeStruct((512,), jnp.int32),
        in_specs=[smem] * 4,
        out_specs=smem,
        scratch_shapes=[pltpu.SMEM((n_depth * results,), jnp.int32)],
        name="pairs",
    )(where, ham_keys, it_keys, aim_keys)
    sent, kept = pl.pallas_call(
        product_kernel,
        out_shape=(halves,) * 2,
        in_specs=[smem] + [anywhere] * 9,
        out_specs=(vmem,) * 2,
        scratch_shapes=[
            pltpu.VMEM((n_depth * results, block, block), jnp.float32),
            pltpu.VMEM((WINDOW, block, block), jnp.bfloat16),
            pltpu.VMEM((WINDOW, block, block), jnp.bfloat16),
            pltpu.SemaphoreType.DMA((WINDOW,)),
            pltpu.SemaphoreType.DMA((WINDOW,)),
        ],
        compiler_params=pltpu.CompilerParams(vmem_limit_bytes=24 << 20),
        name="products",
    )(*[pltpu.with_memory_space_constraint(x, pltpu.HBM) for x in (pairs, iterate)], *hams)
    near = lax.ppermute(sent, "depth", [(d, d ^ 1) for d in range(n_depth)])
    onward = (kept[0].astype(jnp.float32) + near[0].astype(jnp.float32)).astype(jnp.bfloat16)
    far = lax.ppermute(onward, "depth", [(d, d ^ 2) for d in range(n_depth)])
    prior = previous.reshape(results, block, block).astype(jnp.float32)
    live = x_flags.reshape(results, 1, 1).astype(jnp.float32)
    base = 2.0 * (kept[1].astype(jnp.float32) + near[1].astype(jnp.float32)) - prior
    base = lax.optimization_barrier(base)
    result = (base + 2.0 * far.astype(jnp.float32)) * live
    return result.astype(jnp.bfloat16).reshape(previous.shape)


def solution(mesh):
    placed = (
        P("row", "col", "depth", None, None, None),
        P("row", "col", "depth", None),
        P("row", "col", "depth", None),
        P("row", "col", "depth", None),
        P("row", "depth", "col", None, None, None, None),
        P("row", "depth", "col", None, None),
        P("row", "depth", "col", None, None),
        P("row", "depth", "col", None, None, None, None),
    )
    return jax.shard_map(
        body,
        mesh=mesh,
        in_specs=placed,
        out_specs=P("row", "depth", "col", None, None, None, None),
        check_vma=False,
    )
```

```python
import jax
import jax.numpy as jnp
from jax import lax
from jax.experimental import pallas as pl
from jax.experimental.pallas import tpu as pltpu
from jax.sharding import PartitionSpec as P

WINDOW = 16
SLOTS = 12


def key_kernel(*refs):
    hams, shards, (ham_keys, it_keys, ham_slab, it_slab, sem) = refs[:8], refs[8:-5], refs[-5:]
    tail = ham_slab.shape[1]
    n_ham = ham_slab.shape[0]
    copies = []
    for k, ham in enumerate(hams):
        copies.append(pltpu.make_async_copy(ham.at[pl.ds(ham.shape[0] - tail, tail)], ham_slab.at[k], sem.at[k]))
    for k, shard in enumerate(shards):
        shard = shard.at[0] if len(shard.shape) == 3 else shard
        middle = pl.ds((shard.shape[0] - tail) // 2, tail)
        copies.append(pltpu.make_async_copy(shard.at[middle], it_slab.at[k], sem.at[n_ham + k]))
    for copy in copies:
        copy.start()
    for k, copy in enumerate(copies):
        copy.wait()
        if k < n_ham:
            held = ham_slab[k].astype(jnp.float32)
            for t in range(2):
                row, col, flag = (held[3 * t + i : 3 * t + i + 1] for i in range(3))
                place = jnp.where(flag > 0, row * 8 + col, -1.0)
                ham_keys[2 * k + t : 2 * k + t + 1] = place.astype(jnp.int32)
        else:
            held = it_slab[k - n_ham].astype(jnp.float32)
            place = jnp.where(held[1:2] > 0, held[0:1], -1.0)
            it_keys[k - n_ham : k - n_ham + 1] = place.astype(jnp.int32)


def list_tile(tile, hop, count, ham, own_keys, aim, pairs, touched, slots):
    base = tile * SLOTS + hop * 16 * 256

    def live(state):
        slot, _ = state
        return (slot < slots) & (ham[tile, slot] >= 0)

    def one_slot(state):
        slot, count = state
        key = ham[tile, slot]
        row = key // 8
        inner = key % 8
        for w in range(2):
            there = own_keys(inner * 2 + w)
            for v in range(2):
                goal = row * 2 + v
                match = (aim[goal] == there).astype(jnp.int32)
                seen = touched[goal]
                pairs[count] = base + slot + (inner * 2 + w) * 256 + (goal + 64 * seen) * 65536
                touched[goal] = seen | match
                count = count + match
        return slot + 1, count

    return lax.while_loop(live, one_slot, (jnp.int32(0), count))[1]


def pair_kernel(where, ham, iterate, aim, pairs, touched):
    tiles = ham.shape[0]
    pieces = iterate.shape[0] + 1
    last = pieces // 2
    near = where[0] // 4
    step = where[0] % 4
    sign = 1 - 2 * (where[1] % 2)

    def untouch(at, carry):
        touched[at] = 0
        return carry

    lax.fori_loop(0, aim.shape[0], untouch, 0)

    def one_tile(tile, count):
        array = tile // 2
        col = ((array // 4) ^ near) * 4 + (step - array % 4 + 4) % 4
        piece = col * 2 + tile % 2
        hop = (sign * (where[2] - piece) + pieces) % pieces
        at = jnp.minimum(jnp.where(hop > last, hop - 1, hop), pieces - 2)
        keys = lambda spot: iterate[at, spot]
        late = hop == last
        return list_tile(tile, hop, count, ham, keys, aim, pairs, touched, jnp.where(late, 0, SLOTS))

    end = pairs.shape[0]
    pairs[end - 1] = lax.fori_loop(0, tiles, one_tile, jnp.int32(0))
    pairs[end - 2] = where[1]
    piece = (where[2] + last) % pieces
    col = piece // 2
    array = ((col // 4) ^ near) * 4 + (step - col % 4 + 4) % 4
    pairs[end - 3] = array * 2 + piece % 2

    def keep(at, carry):
        pairs[end - 96 + at] = touched[at]
        return carry

    lax.fori_loop(0, aim.shape[0], keep, 0)


def product_kernel(pairs, ham_keys, aim, *rest):
    hams, shards, rest = rest[:8], rest[8:25], rest[25:]
    sent, kept, total, ham_buf, it_buf, slab, key_row, late_keys, late_pairs, touched, ham_sem, it_sem, late_sem = rest
    shards = [shard.at[0] if len(shard.shape) == 3 else shard for shard in shards]
    size = ham_buf.shape[1]
    end = pairs.shape[0]
    count = pairs[end - 1]
    depth = pairs[end - 2]
    core = depth % 2
    high = depth // 2
    last = 8
    tail = slab.shape[0]
    half = sent.shape[1]
    cut = last * size
    slab_at = pl.ds(pl.multiple_of(core * cut, tail), tail)
    slab_copy = pltpu.make_async_copy(shards[last].at[slab_at], slab, late_sem.at[0])
    slab_copy.start()

    def start(codes, at):
        code = codes[at]
        ham_at = code % 256
        spot = (code // 256) % 16
        hop = (code // 4096) % 16
        slot = at % WINDOW
        rows = pl.ds(pl.multiple_of((ham_at % (2 * SLOTS)) * size, size), size)
        for k, ham in enumerate(hams):

            @pl.when(ham_at // (2 * SLOTS) == k)
            def _():
                pltpu.make_async_copy(ham.at[rows], ham_buf.at[slot], ham_sem.at[slot]).start()

        upper = (spot >= 8).astype(jnp.int32)
        split = hop == last
        source = jnp.where(split & (upper == core), 16, hop)
        row = spot * size + tail * upper - jnp.where(split, cut * upper, 0)
        rows = pl.ds(pl.multiple_of(row, tail), size)
        for k, shard in enumerate(shards):

            @pl.when(source == k)
            def _():
                pltpu.make_async_copy(shard.at[rows], it_buf.at[slot], it_sem.at[slot]).start()

    def prime(codes, count):
        def first(at, carry):
            start(codes, at)
            return carry

        lax.fori_loop(0, jnp.minimum(count, WINDOW), first, 0)

    def drain(codes, count):
        def multiply(at, carry):
            slot = at % WINDOW
            pltpu.make_async_copy(hams[0].at[pl.ds(0, size)], ham_buf.at[slot], ham_sem.at[slot]).wait()
            pltpu.make_async_copy(shards[0].at[pl.ds(0, size)], it_buf.at[slot], it_sem.at[slot]).wait()
            goal = codes[at] // 65536
            seen = goal >= 64
            goal = goal % 64
            product = jnp.dot(ham_buf[slot], it_buf[slot], preferred_element_type=jnp.float32)
            product = jnp.where(seen, total[goal], 0.0) + product
            total[goal] = product
            owner = goal // half
            part = (owner // 2 == high).astype(jnp.int32)

            @pl.when(owner % 2 == core)
            def _():
                kept[part, goal % half] = product.astype(kept.dtype)

            @pl.when(owner % 2 != core)
            def _():
                sent[part, goal % half] = product.astype(sent.dtype)

            @pl.when(at + WINDOW < count)
            def _():
                start(codes, at + WINDOW)

            return carry

        lax.fori_loop(0, count, multiply, 0)

    prime(pairs, count)

    def clear(at, carry):
        for part in range(2):
            sent[part, at] = jnp.zeros(sent.shape[2:], sent.dtype)
            kept[part, at] = jnp.zeros(kept.shape[2:], kept.dtype)
        return carry

    lax.fori_loop(0, half, clear, 0, unroll=4)

    def recall(at, carry):
        touched[at] = pairs[end - 96 + at]
        return carry

    slab_copy.wait()
    held = slab[...].astype(jnp.float32)
    key_row[...] = jnp.where(held[1:2] > 0, held[0:1], -1.0).astype(jnp.int32)
    key_copy = pltpu.make_async_copy(key_row, late_keys, late_sem.at[1])
    key_copy.start()
    lax.fori_loop(0, aim.shape[0], recall, 0)
    drain(pairs, count)
    key_copy.wait()
    keys = lambda spot: late_keys[0, spot]
    late = list_tile(pairs[end - 3], last, jnp.int32(0), ham_keys, keys, aim, late_pairs, touched, SLOTS)
    prime(late_pairs, late)
    drain(late_pairs, late)


def with_slab(blocks, ints, at):
    width = blocks.shape[-1]
    ints = ints.astype(blocks.dtype)
    ints = jnp.pad(ints, ((0, 16 - ints.shape[0]), (0, width - ints.shape[1])))
    rows = blocks.reshape(-1, width)
    return jnp.concatenate([rows[: at * width], ints, rows[at * width :]], axis=0)


def body(h_blocks, h_rows, h_cols, h_flags, x_blocks, x_cols, x_flags, previous):
    block = x_blocks.shape[-1]
    n_row, n_col, n_depth = lax.axis_size("row"), lax.axis_size("col"), lax.axis_size("depth")
    results = x_cols.shape[3] * x_cols.shape[4]
    where = jnp.stack([lax.axis_index("col"), lax.axis_index("depth"), lax.axis_index("row")]).astype(jnp.int32)
    x_ints = jnp.concatenate([x_cols.reshape(1, -1), x_flags.reshape(1, -1)], axis=0)
    own = with_slab(x_blocks, x_ints, results // 2)
    h_ints = jnp.concatenate([h_rows, h_cols, h_flags], axis=2).reshape(-1, SLOTS)
    mine = with_slab(h_blocks, h_ints, 2 * SLOTS)

    last = n_row // 2
    cut = results // 2 * block
    core = lax.axis_index("depth") % 2
    swap = [(d, d ^ 1) for d in range(n_depth)]
    ring = []
    for r in range(n_row):
        for d in range(n_depth):
            ring.append((r * n_depth + d, (r + 1 - 2 * (d % 2)) % n_row * n_depth + d))

    beside = lax.ppermute(mine, "col", [(c, c ^ 4) for c in range(n_col)])
    pattern = jnp.concatenate([x_cols, x_flags], axis=2)
    beside, pattern = lax.optimization_barrier((beside, pattern))
    aim_ints = lax.all_gather(pattern, "depth", axis=1, tiled=True)
    ahead = [(c, (c // 4) * 4 + (c + 1) % 4) for c in range(n_col)]
    back = [(c, (c // 4) * 4 + (c + 3) % 4) for c in range(n_col)]
    hams = [mine, None, None, None, beside, None, None, None]
    hams[1] = lax.ppermute(mine, "col", ahead)
    hams[3] = lax.ppermute(mine, "col", back)
    hams[5] = lax.ppermute(beside, "col", ahead)
    hams[7] = lax.ppermute(beside, "col", back)

    pair = jnp.stack([own, lax.ppermute(own, "depth", swap)])
    shards = [own] + [None] * n_row
    for hop in range(1, last):
        pair = lax.ppermute(pair, ("row", "depth"), ring)
        if hop == 1:
            pair, hams[4] = lax.optimization_barrier((pair, hams[4]))
        if hop == 2:
            pair, aim_ints, hams[1], hams[3] = lax.optimization_barrier((pair, aim_ints, hams[1], hams[3]))
            hams[2] = lax.ppermute(hams[1], "col", ahead)
        if hop == 4:
            pair, hams[5], hams[7] = lax.optimization_barrier((pair, hams[5], hams[7]))
            hams[6] = lax.ppermute(hams[7], "col", back)
        if hop == last - 2:
            pair, hams[2], hams[6] = lax.optimization_barrier((pair, hams[2], hams[6]))
        if hop > 2:
            before = n_row - hop + 2
            pair, shards[before] = lax.optimization_barrier((pair, shards[before]))
        shards[hop] = pair
        shards[n_row - hop] = lax.ppermute(pair[1], "depth", swap)
    portion = lax.dynamic_slice_in_dim(pair, (1 - core) * cut, cut + 16, axis=1)
    shards[last] = lax.ppermute(portion, ("row", "depth"), ring)
    shards[last], *_ = lax.optimization_barrier((shards[last], shards[last + 1], shards[last + 2]))
    shards[n_row] = lax.ppermute(shards[last][1], "depth", swap)
    hams, shards = ([pltpu.with_memory_space_constraint(x, pltpu.HBM) for x in xs] for xs in (hams, shards))

    aim_keys = jnp.where(aim_ints[0, :, 1] > 0, aim_ints[0, :, 0], -2).reshape(-1)
    smem = pl.BlockSpec(memory_space=pltpu.SMEM)
    anywhere = pl.BlockSpec(memory_space=pl.ANY)
    vmem = pl.BlockSpec(memory_space=pltpu.VMEM)
    early = shards[:last] + shards[last + 1 : n_row]
    ham_keys, it_keys = pl.pallas_call(
        key_kernel,
        out_shape=(
            jax.ShapeDtypeStruct((2 * n_col, block), jnp.int32),
            jax.ShapeDtypeStruct((len(early), block), jnp.int32),
        ),
        in_specs=[anywhere] * (len(hams) + len(early)),
        out_specs=(vmem, vmem),
        scratch_shapes=[
            pltpu.VMEM((n_col, 16, block), jnp.bfloat16),
            pltpu.VMEM((len(early), 16, block), jnp.bfloat16),
            pltpu.SemaphoreType.DMA((n_col + len(early),)),
        ],
        name="keys",
    )(*hams, *early)
    pairs = pl.pallas_call(
        pair_kernel,
        out_shape=jax.ShapeDtypeStruct((512,), jnp.int32),
        in_specs=[smem] * 4,
        out_specs=smem,
        scratch_shapes=[pltpu.SMEM((n_depth * results,), jnp.int32)],
        name="pairs",
    )(where, ham_keys, it_keys, aim_keys)
    halves = jax.ShapeDtypeStruct((2, results, block, block), jnp.bfloat16)
    sent, kept = pl.pallas_call(
        product_kernel,
        out_shape=(halves,) * 2,
        in_specs=[smem] * 3 + [anywhere] * (len(hams) + n_row + 1),
        out_specs=(vmem,) * 2,
        scratch_shapes=[
            pltpu.VMEM((n_depth * results, block, block), jnp.float32),
            pltpu.VMEM((WINDOW, block, block), jnp.bfloat16),
            pltpu.VMEM((WINDOW, block, block), jnp.bfloat16),
            pltpu.VMEM((16, block), jnp.bfloat16),
            pltpu.VMEM((1, block), jnp.int32),
            pltpu.SMEM((1, block), jnp.int32),
            pltpu.SMEM((64,), jnp.int32),
            pltpu.SMEM((64,), jnp.int32),
            pltpu.SemaphoreType.DMA((WINDOW,)),
            pltpu.SemaphoreType.DMA((WINDOW,)),
            pltpu.SemaphoreType.DMA((2,)),
        ],
        compiler_params=pltpu.CompilerParams(vmem_limit_bytes=24 << 20),
        name="products",
    )(*[pltpu.with_memory_space_constraint(x, pltpu.HBM) for x in (pairs, ham_keys, aim_keys)], *hams, *shards)
    near = lax.ppermute(sent, "depth", [(d, d ^ 1) for d in range(n_depth)])
    onward = (kept[0].astype(jnp.float32) + near[0].astype(jnp.float32)).astype(jnp.bfloat16)
    far = lax.ppermute(onward, "depth", [(d, d ^ 2) for d in range(n_depth)])
    prior = previous.reshape(results, block, block).astype(jnp.float32)
    live = x_flags.reshape(results, 1, 1).astype(jnp.float32)
    base = 2.0 * (kept[1].astype(jnp.float32) + near[1].astype(jnp.float32)) - prior
    base = lax.optimization_barrier(base)
    result = (base + 2.0 * far.astype(jnp.float32)) * live
    return result.astype(jnp.bfloat16).reshape(previous.shape)


def solution(mesh):
    placed = (
        P("row", "col", "depth", None, None, None),
        P("row", "col", "depth", None),
        P("row", "col", "depth", None),
        P("row", "col", "depth", None),
        P("row", "depth", "col", None, None, None, None),
        P("row", "depth", "col", None, None),
        P("row", "depth", "col", None, None),
        P("row", "depth", "col", None, None, None, None),
    )
    return jax.shard_map(
        body,
        mesh=mesh,
        in_specs=placed,
        out_specs=P("row", "depth", "col", None, None, None, None),
        check_vma=False,
    )
```

```python
import jax
import jax.numpy as jnp
from jax import lax
from jax.experimental import pallas as pl
from jax.experimental.pallas import tpu as pltpu
from jax.sharding import PartitionSpec as P

WINDOW = 16


def key_kernel(*refs):
    hams, (keys, slab, sem) = refs[:8], refs[8:]
    tail = slab.shape[1]
    copies = [
        pltpu.make_async_copy(ham.at[pl.ds(ham.shape[0] - tail, tail)], slab.at[k], sem.at[k])
        for k, ham in enumerate(hams)
    ]
    for copy in copies:
        copy.start()
    for k, copy in enumerate(copies):
        copy.wait()
        held = slab[k].astype(jnp.float32)
        for t in range(2):
            row, col, flag = (held[3 * t + i : 3 * t + i + 1] for i in range(3))
            place = jnp.where(flag > 0, row * 8 + col, -1.0)
            keys[2 * k + t : 2 * k + t + 1] = place.astype(jnp.int32)


def pair_kernel(where, ham, iterate, aim, pairs, touched):
    def untouch(at, carry):
        touched[at] = 0
        return carry

    lax.fori_loop(0, aim.shape[0], untouch, 0)
    pieces = ham.shape[0]
    slots = 12
    per_col = pieces // 8
    width = iterate.shape[1]
    near = where[0] // 4
    step = where[0] % 4

    def one_tile(tile, count):
        array = tile // per_col
        col = ((array // 4) ^ near) * 4 + (step - array % 4 + 4) % 4
        piece = col * per_col + tile % per_col
        base = tile * slots + piece * width * 256

        def live(state):
            slot, _ = state
            return (slot < slots) & (ham[tile, slot] >= 0)

        def one_slot(state):
            slot, count = state
            key = ham[tile, slot]
            row = key // 8
            inner = key % 8
            for w in range(2):
                there = iterate[piece, inner * 2 + w]
                for v in range(2):
                    goal = row * 2 + v
                    match = (aim[goal] == there).astype(jnp.int32)
                    seen = touched[goal]
                    pairs[count] = base + slot + (inner * 2 + w) * 256 + (goal + 64 * seen) * 65536
                    touched[goal] = seen | match
                    count = count + match
            return slot + 1, count

        return lax.while_loop(live, one_slot, (jnp.int32(0), count))[1]

    pairs[pairs.shape[0] - 1] = lax.fori_loop(0, pieces, one_tile, jnp.int32(0))
    pairs[pairs.shape[0] - 2] = where[1]


def product_kernel(pairs, iterate, *rest):
    hams, (sent_on, sent_keep, kept, total, ham_buf, it_buf, ham_sem, it_sem) = rest[:8], rest[8:]
    size = ham_buf.shape[1]
    slots = hams[0].shape[0] // size
    count = pairs[pairs.shape[0] - 1]

    def start(at):
        code = pairs[at]
        ham_at = code % 256
        slot = at % WINDOW
        rows = pl.ds(pl.multiple_of((ham_at % slots) * size, size), size)
        for k, ham in enumerate(hams):

            @pl.when(ham_at // slots == k)
            def _():
                pltpu.make_async_copy(ham.at[rows], ham_buf.at[slot], ham_sem.at[slot]).start()

        pltpu.make_async_copy(iterate.at[(code // 256) % 256], it_buf.at[slot], it_sem.at[slot]).start()

    def first(at, carry):
        start(at)
        return carry

    lax.fori_loop(0, jnp.minimum(count, WINDOW), first, 0)

    half = kept.shape[1]
    depth = pairs[pairs.shape[0] - 2]
    core = depth % 2
    high = depth // 2

    def clear(at, carry):
        for ref in (sent_on.at[at], sent_keep.at[at], kept.at[0, at], kept.at[1, at]):
            ref[...] = jnp.zeros(ref.shape, ref.dtype)
        return carry

    lax.fori_loop(0, half, clear, 0, unroll=4)

    def multiply(at, carry):
        slot = at % WINDOW
        pltpu.make_async_copy(hams[0].at[pl.ds(0, size)], ham_buf.at[slot], ham_sem.at[slot]).wait()
        pltpu.make_async_copy(iterate.at[0], it_buf.at[slot], it_sem.at[slot]).wait()
        goal = pairs[at] // 65536
        seen = goal >= 64
        goal = goal % 64
        product = jnp.dot(ham_buf[slot], it_buf[slot], preferred_element_type=jnp.float32)
        product = jnp.where(seen, total[goal], 0.0) + product
        total[goal] = product
        owner = goal // half
        part = (owner // 2 == high).astype(jnp.int32)

        @pl.when(owner % 2 == core)
        def _():
            kept[part, goal % half] = product.astype(kept.dtype)

        @pl.when((owner % 2 != core) & (part == 0))
        def _():
            sent_on[goal % half] = product.astype(sent_on.dtype)

        @pl.when((owner % 2 != core) & (part == 1))
        def _():
            sent_keep[goal % half] = product.astype(sent_keep.dtype)

        @pl.when(at + WINDOW < count)
        def _():
            start(at + WINDOW)

        return carry

    lax.fori_loop(0, count, multiply, 0)


def body(h_blocks, h_rows, h_cols, h_flags, x_blocks, x_cols, x_flags, previous):
    block = x_blocks.shape[-1]
    n_row, n_col, n_depth = lax.axis_size("row"), lax.axis_size("col"), lax.axis_size("depth")
    where = jnp.stack([lax.axis_index("col"), lax.axis_index("depth")]).astype(jnp.int32)
    iterate = lax.all_gather(x_blocks[0, 0, 0], "row", axis=0)
    iterate = iterate.reshape(-1, block, block)
    it_ints = jnp.concatenate([x_cols, x_flags], axis=2)
    aim_ints = lax.all_gather(it_ints, "depth", axis=1, tiled=True)
    slots = h_rows.shape[-1]
    ham_ints = jnp.concatenate([h_rows, h_cols, h_flags], axis=2).reshape(-1, slots)
    ham_ints = ham_ints.astype(jnp.bfloat16)
    ham_ints = jnp.pad(ham_ints, ((0, 16 - ham_ints.shape[0]), (0, block - slots)))
    mine = jnp.concatenate([h_blocks.reshape(-1, block), ham_ints], axis=0)

    def send(source, flip, step):
        route = [(c, ((c // 4) ^ flip) * 4 + (c % 4 + step) % 4) for c in range(n_col)]
        return lax.ppermute(source, "col", route)

    hams = [mine] + [None] * (n_col - 1)
    for flip, step in ((0, 1), (0, 3)):
        hams[flip * 4 + step] = send(mine, flip, step)
    crossing, aim_ints = lax.optimization_barrier((mine, aim_ints))
    for flip, step in ((1, 0), (1, 2), (1, 1)):
        hams[flip * 4 + step] = send(crossing, flip, step)
    hams[1], crossing = lax.optimization_barrier((hams[1], crossing))
    hams[7] = send(crossing, 1, 3)
    hams[3], crossing, it_ints = lax.optimization_barrier((hams[3], crossing, it_ints))
    hams[2] = send(crossing, 0, 2)
    it_ints = lax.all_gather(it_ints, "row", axis=0, tiled=True)
    hams = [pltpu.with_memory_space_constraint(ham, pltpu.HBM) for ham in hams]
    it_keys = jnp.where(it_ints[:, 0, 1] > 0, it_ints[:, 0, 0], -1).reshape(n_row, -1)
    aim_keys = jnp.where(aim_ints[0, :, 1] > 0, aim_ints[0, :, 0], -2).reshape(-1)
    smem = pl.BlockSpec(memory_space=pltpu.SMEM)
    anywhere = pl.BlockSpec(memory_space=pl.ANY)
    vmem = pl.BlockSpec(memory_space=pltpu.VMEM)
    ham_keys = pl.pallas_call(
        key_kernel,
        out_shape=jax.ShapeDtypeStruct((n_row, block), jnp.int32),
        in_specs=[anywhere] * n_col,
        out_specs=vmem,
        scratch_shapes=[pltpu.VMEM((n_col, 16, block), jnp.bfloat16), pltpu.SemaphoreType.DMA((n_col,))],
        name="keys",
    )(*hams)
    results = x_cols.shape[3] * x_cols.shape[4]
    halves = jax.ShapeDtypeStruct((2, results, block, block), jnp.bfloat16)
    pairs = pl.pallas_call(
        pair_kernel,
        out_shape=jax.ShapeDtypeStruct((512,), jnp.int32),
        in_specs=[smem] * 4,
        out_specs=smem,
        scratch_shapes=[pltpu.SMEM((n_depth * results,), jnp.int32)],
        name="pairs",
    )(where, ham_keys, it_keys, aim_keys)
    whole = jax.ShapeDtypeStruct((results, block, block), jnp.bfloat16)
    sent_on, sent_keep, kept = pl.pallas_call(
        product_kernel,
        out_shape=(whole, whole, halves),
        in_specs=[smem] + [anywhere] * 9,
        out_specs=(vmem,) * 3,
        scratch_shapes=[
            pltpu.VMEM((n_depth * results, block, block), jnp.float32),
            pltpu.VMEM((WINDOW, block, block), jnp.bfloat16),
            pltpu.VMEM((WINDOW, block, block), jnp.bfloat16),
            pltpu.SemaphoreType.DMA((WINDOW,)),
            pltpu.SemaphoreType.DMA((WINDOW,)),
        ],
        compiler_params=pltpu.CompilerParams(vmem_limit_bytes=24 << 20),
        name="products",
    )(*[pltpu.with_memory_space_constraint(x, pltpu.HBM) for x in (pairs, iterate)], *hams)
    to_core = [(d, d ^ 1) for d in range(n_depth)]
    near_on = lax.ppermute(sent_on, "depth", to_core)
    near_keep = lax.ppermute(sent_keep, "depth", to_core)
    far = []
    for rows in (slice(0, results // 2), slice(results // 2, results)):
        onward = kept[0, rows].astype(jnp.float32) + near_on[rows].astype(jnp.float32)
        far.append(lax.ppermute(onward.astype(jnp.bfloat16), "depth", [(d, d ^ 2) for d in range(n_depth)]))
    far = jnp.concatenate(far, axis=0)
    prior = previous.reshape(results, block, block).astype(jnp.float32)
    live = x_flags.reshape(results, 1, 1).astype(jnp.float32)
    base = 2.0 * (kept[1].astype(jnp.float32) + near_keep.astype(jnp.float32)) - prior
    base = lax.optimization_barrier(base)
    result = (base + 2.0 * far.astype(jnp.float32)) * live
    return result.astype(jnp.bfloat16).reshape(previous.shape)


def solution(mesh):
    placed = (
        P("row", "col", "depth", None, None, None),
        P("row", "col", "depth", None),
        P("row", "col", "depth", None),
        P("row", "col", "depth", None),
        P("row", "depth", "col", None, None, None, None),
        P("row", "depth", "col", None, None),
        P("row", "depth", "col", None, None),
        P("row", "depth", "col", None, None, None, None),
    )
    return jax.shard_map(
        body,
        mesh=mesh,
        in_specs=placed,
        out_specs=P("row", "depth", "col", None, None, None, None),
        check_vma=False,
    )
```

```python
import jax
import jax.numpy as jnp
from jax import lax
from jax.experimental import pallas as pl
from jax.experimental.pallas import tpu as pltpu
from jax.sharding import PartitionSpec as P

WINDOW = 16


def key_kernel(*refs):
    hams, (keys, slab, sem) = refs[:8], refs[8:]
    tail = slab.shape[1]
    copies = [
        pltpu.make_async_copy(ham.at[pl.ds(ham.shape[0] - tail, tail)], slab.at[k], sem.at[k])
        for k, ham in enumerate(hams)
    ]
    for copy in copies:
        copy.start()
    for k, copy in enumerate(copies):
        copy.wait()
        held = slab[k].astype(jnp.float32)
        for t in range(2):
            row, col, flag = (held[3 * t + i : 3 * t + i + 1] for i in range(3))
            place = jnp.where(flag > 0, row * 8 + col, -1.0)
            keys[2 * k + t : 2 * k + t + 1] = place.astype(jnp.int32)


def pair_kernel(where, ham, iterate, aim, pairs, touched):
    def untouch(at, carry):
        touched[at] = 0
        return carry

    lax.fori_loop(0, aim.shape[0], untouch, 0)
    pieces = ham.shape[0]
    slots = 12
    per_col = pieces // 8
    width = iterate.shape[1]
    near = where[0] // 4
    step = where[0] % 4

    def one_tile(tile, count):
        array = tile // per_col
        col = ((array // 4) ^ near) * 4 + (step - array % 4 + 4) % 4
        piece = col * per_col + tile % per_col
        base = tile * slots + piece * width * 256

        def live(state):
            slot, _ = state
            return (slot < slots) & (ham[tile, slot] >= 0)

        def one_slot(state):
            slot, count = state
            key = ham[tile, slot]
            row = key // 8
            inner = key % 8
            for w in range(2):
                there = iterate[piece, inner * 2 + w]
                for v in range(2):
                    goal = row * 2 + v
                    match = (aim[goal] == there).astype(jnp.int32)
                    seen = touched[goal]
                    pairs[count] = base + slot + (inner * 2 + w) * 256 + (goal + 64 * seen) * 65536
                    touched[goal] = seen | match
                    count = count + match
            return slot + 1, count

        return lax.while_loop(live, one_slot, (jnp.int32(0), count))[1]

    pairs[pairs.shape[0] - 1] = lax.fori_loop(0, pieces, one_tile, jnp.int32(0))
    pairs[pairs.shape[0] - 2] = where[1]


def product_kernel(pairs, iterate, *rest):
    hams, (sent, kept, total, ham_buf, it_buf, ham_sem, it_sem) = rest[:8], rest[8:]
    size = ham_buf.shape[1]
    slots = hams[0].shape[0] // size
    count = pairs[pairs.shape[0] - 1]

    def start(at):
        code = pairs[at]
        ham_at = code % 256
        slot = at % WINDOW
        rows = pl.ds(pl.multiple_of((ham_at % slots) * size, size), size)
        for k, ham in enumerate(hams):

            @pl.when(ham_at // slots == k)
            def _():
                pltpu.make_async_copy(ham.at[rows], ham_buf.at[slot], ham_sem.at[slot]).start()

        pltpu.make_async_copy(iterate.at[(code // 256) % 256], it_buf.at[slot], it_sem.at[slot]).start()

    def first(at, carry):
        start(at)
        return carry

    lax.fori_loop(0, jnp.minimum(count, WINDOW), first, 0)

    half = sent.shape[1]
    depth = pairs[pairs.shape[0] - 2]
    core = depth % 2
    high = depth // 2

    def clear(at, carry):
        for part in range(2):
            sent[part, at] = jnp.zeros(sent.shape[2:], sent.dtype)
            kept[part, at] = jnp.zeros(kept.shape[2:], kept.dtype)
        return carry

    lax.fori_loop(0, half, clear, 0, unroll=4)

    def arrive(at):
        slot = at % WINDOW
        pltpu.make_async_copy(hams[0].at[pl.ds(0, size)], ham_buf.at[slot], ham_sem.at[slot]).wait()
        pltpu.make_async_copy(iterate.at[0], it_buf.at[slot], it_sem.at[slot]).wait()

    def store(at, product):
        goal = pairs[at] // 65536
        seen = goal >= 64
        goal = goal % 64
        product = jnp.where(seen, total[goal], 0.0) + product
        total[goal] = product
        owner = goal // half
        part = (owner // 2 == high).astype(jnp.int32)

        @pl.when(owner % 2 == core)
        def _():
            kept[part, goal % half] = product.astype(kept.dtype)

        @pl.when(owner % 2 != core)
        def _():
            sent[part, goal % half] = product.astype(sent.dtype)

        @pl.when(at + WINDOW < count)
        def _():
            start(at + WINDOW)

    def two(step, carry):
        at = 2 * step
        more = at + 1 < count
        arrive(at)

        @pl.when(more)
        def _():
            arrive(at + 1)

        slots_now = (at % WINDOW, (at + 1) % WINDOW)
        products = [jnp.dot(ham_buf[k], it_buf[k], preferred_element_type=jnp.float32) for k in slots_now]
        store(at, products[0])

        @pl.when(more)
        def _():
            store(at + 1, products[1])

        return carry

    lax.fori_loop(0, (count + 1) // 2, two, 0)


def body(h_blocks, h_rows, h_cols, h_flags, x_blocks, x_cols, x_flags, previous):
    block = x_blocks.shape[-1]
    n_row, n_col, n_depth = lax.axis_size("row"), lax.axis_size("col"), lax.axis_size("depth")
    where = jnp.stack([lax.axis_index("col"), lax.axis_index("depth")]).astype(jnp.int32)
    iterate = lax.all_gather(x_blocks[0, 0, 0], "row", axis=0)
    iterate = iterate.reshape(-1, block, block)
    it_ints = jnp.concatenate([x_cols, x_flags], axis=2)
    aim_ints = lax.all_gather(it_ints, "depth", axis=1, tiled=True)
    slots = h_rows.shape[-1]
    ham_ints = jnp.concatenate([h_rows, h_cols, h_flags], axis=2).reshape(-1, slots)
    ham_ints = ham_ints.astype(jnp.bfloat16)
    ham_ints = jnp.pad(ham_ints, ((0, 16 - ham_ints.shape[0]), (0, block - slots)))
    mine = jnp.concatenate([h_blocks.reshape(-1, block), ham_ints], axis=0)

    def send(source, flip, step):
        route = [(c, ((c // 4) ^ flip) * 4 + (c % 4 + step) % 4) for c in range(n_col)]
        return lax.ppermute(source, "col", route)

    hams = [mine] + [None] * (n_col - 1)
    for flip, step in ((0, 1), (0, 3)):
        hams[flip * 4 + step] = send(mine, flip, step)
    crossing, aim_ints = lax.optimization_barrier((mine, aim_ints))
    for flip, step in ((1, 0), (1, 2), (1, 1)):
        hams[flip * 4 + step] = send(crossing, flip, step)
    hams[1], crossing = lax.optimization_barrier((hams[1], crossing))
    hams[7] = send(crossing, 1, 3)
    hams[3], crossing, it_ints = lax.optimization_barrier((hams[3], crossing, it_ints))
    hams[2] = send(crossing, 0, 2)
    it_ints = lax.all_gather(it_ints, "row", axis=0, tiled=True)
    hams = [pltpu.with_memory_space_constraint(ham, pltpu.HBM) for ham in hams]
    it_keys = jnp.where(it_ints[:, 0, 1] > 0, it_ints[:, 0, 0], -1).reshape(n_row, -1)
    aim_keys = jnp.where(aim_ints[0, :, 1] > 0, aim_ints[0, :, 0], -2).reshape(-1)
    smem = pl.BlockSpec(memory_space=pltpu.SMEM)
    anywhere = pl.BlockSpec(memory_space=pl.ANY)
    vmem = pl.BlockSpec(memory_space=pltpu.VMEM)
    ham_keys = pl.pallas_call(
        key_kernel,
        out_shape=jax.ShapeDtypeStruct((n_row, block), jnp.int32),
        in_specs=[anywhere] * n_col,
        out_specs=vmem,
        scratch_shapes=[pltpu.VMEM((n_col, 16, block), jnp.bfloat16), pltpu.SemaphoreType.DMA((n_col,))],
        name="keys",
    )(*hams)
    results = x_cols.shape[3] * x_cols.shape[4]
    halves = jax.ShapeDtypeStruct((2, results, block, block), jnp.bfloat16)
    pairs = pl.pallas_call(
        pair_kernel,
        out_shape=jax.ShapeDtypeStruct((512,), jnp.int32),
        in_specs=[smem] * 4,
        out_specs=smem,
        scratch_shapes=[pltpu.SMEM((n_depth * results,), jnp.int32)],
        name="pairs",
    )(where, ham_keys, it_keys, aim_keys)
    sent, kept = pl.pallas_call(
        product_kernel,
        out_shape=(halves,) * 2,
        in_specs=[smem] + [anywhere] * 9,
        out_specs=(vmem,) * 2,
        scratch_shapes=[
            pltpu.VMEM((n_depth * results, block, block), jnp.float32),
            pltpu.VMEM((WINDOW, block, block), jnp.bfloat16),
            pltpu.VMEM((WINDOW, block, block), jnp.bfloat16),
            pltpu.SemaphoreType.DMA((WINDOW,)),
            pltpu.SemaphoreType.DMA((WINDOW,)),
        ],
        compiler_params=pltpu.CompilerParams(vmem_limit_bytes=24 << 20),
        name="products",
    )(*[pltpu.with_memory_space_constraint(x, pltpu.HBM) for x in (pairs, iterate)], *hams)
    near = lax.ppermute(sent, "depth", [(d, d ^ 1) for d in range(n_depth)])
    onward = (kept[0].astype(jnp.float32) + near[0].astype(jnp.float32)).astype(jnp.bfloat16)
    far = lax.ppermute(onward, "depth", [(d, d ^ 2) for d in range(n_depth)])
    prior = previous.reshape(results, block, block).astype(jnp.float32)
    live = x_flags.reshape(results, 1, 1).astype(jnp.float32)
    base = 2.0 * (kept[1].astype(jnp.float32) + near[1].astype(jnp.float32)) - prior
    base = lax.optimization_barrier(base)
    result = (base + 2.0 * far.astype(jnp.float32)) * live
    return result.astype(jnp.bfloat16).reshape(previous.shape)


def solution(mesh):
    placed = (
        P("row", "col", "depth", None, None, None),
        P("row", "col", "depth", None),
        P("row", "col", "depth", None),
        P("row", "col", "depth", None),
        P("row", "depth", "col", None, None, None, None),
        P("row", "depth", "col", None, None),
        P("row", "depth", "col", None, None),
        P("row", "depth", "col", None, None, None, None),
    )
    return jax.shard_map(
        body,
        mesh=mesh,
        in_specs=placed,
        out_specs=P("row", "depth", "col", None, None, None, None),
        check_vma=False,
    )
```

```python
import jax
import jax.numpy as jnp
from jax import lax
from jax.experimental import pallas as pl
from jax.experimental.pallas import tpu as pltpu
from jax.sharding import PartitionSpec as P

WINDOW = 16


def key_kernel(*refs):
    hams, (keys, slab, sem) = refs[:8], refs[8:]
    tail = slab.shape[1]
    copies = [
        pltpu.make_async_copy(ham.at[pl.ds(ham.shape[0] - tail, tail)], slab.at[k], sem.at[k])
        for k, ham in enumerate(hams)
    ]
    for copy in copies:
        copy.start()
    for k, copy in enumerate(copies):
        copy.wait()
        held = slab[k].astype(jnp.float32)
        for t in range(2):
            row, col, flag = (held[3 * t + i : 3 * t + i + 1] for i in range(3))
            place = jnp.where(flag > 0, row * 8 + col, -1.0)
            keys[2 * k + t : 2 * k + t + 1] = place.astype(jnp.int32)


def pair_kernel(where, ham, iterate, aim, pairs, touched):
    def untouch(at, carry):
        touched[at] = 0
        return carry

    lax.fori_loop(0, aim.shape[0], untouch, 0)
    pieces = ham.shape[0]
    slots = 12
    per_col = pieces // 8
    width = iterate.shape[1]
    near = where[0] // 4
    step = where[0] % 4

    def one_tile(tile, count):
        array = tile // per_col
        col = ((array // 4) ^ near) * 4 + (step - array % 4 + 4) % 4
        piece = col * per_col + tile % per_col
        base = tile * slots + piece * width * 256

        def live(state):
            slot, _ = state
            return (slot < slots) & (ham[tile, slot] >= 0)

        def one_slot(state):
            slot, count = state
            key = ham[tile, slot]
            row = key // 8
            inner = key % 8
            for w in range(2):
                there = iterate[piece, inner * 2 + w]
                for v in range(2):
                    goal = row * 2 + v
                    match = (aim[goal] == there).astype(jnp.int32)
                    seen = touched[goal]
                    pairs[count] = base + slot + (inner * 2 + w) * 256 + (goal + 64 * seen) * 65536
                    touched[goal] = seen | match
                    count = count + match
            return slot + 1, count

        return lax.while_loop(live, one_slot, (jnp.int32(0), count))[1]

    pairs[pairs.shape[0] - 1] = lax.fori_loop(0, pieces, one_tile, jnp.int32(0))
    pairs[pairs.shape[0] - 2] = where[1]


def product_kernel(pairs, iterate, *rest):
    hams, (sent_on, sent_keep, kept, total, ham_buf, it_buf, ham_sem, it_sem) = rest[:8], rest[8:]
    size = ham_buf.shape[1]
    slots = hams[0].shape[0] // size
    count = pairs[pairs.shape[0] - 1]

    def start(at):
        code = pairs[at]
        ham_at = code % 256
        slot = at % WINDOW
        rows = pl.ds(pl.multiple_of((ham_at % slots) * size, size), size)
        for k, ham in enumerate(hams):

            @pl.when(ham_at // slots == k)
            def _():
                pltpu.make_async_copy(ham.at[rows], ham_buf.at[slot], ham_sem.at[slot]).start()

        pltpu.make_async_copy(iterate.at[(code // 256) % 256], it_buf.at[slot], it_sem.at[slot]).start()

    def first(at, carry):
        start(at)
        return carry

    lax.fori_loop(0, jnp.minimum(count, WINDOW), first, 0)

    half = kept.shape[1]
    depth = pairs[pairs.shape[0] - 2]
    core = depth % 2
    high = depth // 2

    def clear(at, carry):
        for ref in (sent_on.at[at], sent_keep.at[at], kept.at[0, at], kept.at[1, at]):
            ref[...] = jnp.zeros(ref.shape, ref.dtype)
        return carry

    lax.fori_loop(0, half, clear, 0, unroll=4)

    def multiply(at, carry):
        slot = at % WINDOW
        pltpu.make_async_copy(hams[0].at[pl.ds(0, size)], ham_buf.at[slot], ham_sem.at[slot]).wait()
        pltpu.make_async_copy(iterate.at[0], it_buf.at[slot], it_sem.at[slot]).wait()
        goal = pairs[at] // 65536
        seen = goal >= 64
        goal = goal % 64
        product = jnp.dot(ham_buf[slot], it_buf[slot], preferred_element_type=jnp.float32)
        product = jnp.where(seen, total[goal], 0.0) + product
        total[goal] = product
        owner = goal // half
        part = (owner // 2 == high).astype(jnp.int32)

        @pl.when(owner % 2 == core)
        def _():
            kept[part, goal % half] = product.astype(kept.dtype)

        @pl.when((owner % 2 != core) & (part == 0))
        def _():
            sent_on[goal % half] = product.astype(sent_on.dtype)

        @pl.when((owner % 2 != core) & (part == 1))
        def _():
            sent_keep[goal % half] = product.astype(sent_keep.dtype)

        @pl.when(at + WINDOW < count)
        def _():
            start(at + WINDOW)

        return carry

    lax.fori_loop(0, count, multiply, 0)


def body(h_blocks, h_rows, h_cols, h_flags, x_blocks, x_cols, x_flags, previous):
    block = x_blocks.shape[-1]
    n_row, n_col, n_depth = lax.axis_size("row"), lax.axis_size("col"), lax.axis_size("depth")
    where = jnp.stack([lax.axis_index("col"), lax.axis_index("depth")]).astype(jnp.int32)
    iterate = lax.all_gather(x_blocks[0, 0, 0], "row", axis=0)
    iterate = iterate.reshape(-1, block, block)
    it_ints = jnp.concatenate([x_cols, x_flags], axis=2)
    aim_ints = lax.all_gather(it_ints, "depth", axis=1, tiled=True)
    slots = h_rows.shape[-1]
    ham_ints = jnp.concatenate([h_rows, h_cols, h_flags], axis=2).reshape(-1, slots)
    ham_ints = ham_ints.astype(jnp.bfloat16)
    ham_ints = jnp.pad(ham_ints, ((0, 16 - ham_ints.shape[0]), (0, block - slots)))
    mine = jnp.concatenate([h_blocks.reshape(-1, block), ham_ints], axis=0)

    def send(source, flip, step):
        route = [(c, ((c // 4) ^ flip) * 4 + (c % 4 + step) % 4) for c in range(n_col)]
        return lax.ppermute(source, "col", route)

    hams = [mine] + [None] * (n_col - 1)
    for flip, step in ((0, 1), (0, 3)):
        hams[flip * 4 + step] = send(mine, flip, step)
    crossing, aim_ints = lax.optimization_barrier((mine, aim_ints))
    for flip, step in ((1, 0), (1, 2), (1, 1)):
        hams[flip * 4 + step] = send(crossing, flip, step)
    hams[1], crossing = lax.optimization_barrier((hams[1], crossing))
    hams[7] = send(crossing, 1, 3)
    hams[3], crossing, it_ints = lax.optimization_barrier((hams[3], crossing, it_ints))
    hams[2] = send(crossing, 0, 2)
    it_ints = lax.all_gather(it_ints, "row", axis=0, tiled=True)
    hams = [pltpu.with_memory_space_constraint(ham, pltpu.HBM) for ham in hams]
    it_keys = jnp.where(it_ints[:, 0, 1] > 0, it_ints[:, 0, 0], -1).reshape(n_row, -1)
    aim_keys = jnp.where(aim_ints[0, :, 1] > 0, aim_ints[0, :, 0], -2).reshape(-1)
    smem = pl.BlockSpec(memory_space=pltpu.SMEM)
    anywhere = pl.BlockSpec(memory_space=pl.ANY)
    vmem = pl.BlockSpec(memory_space=pltpu.VMEM)
    ham_keys = pl.pallas_call(
        key_kernel,
        out_shape=jax.ShapeDtypeStruct((n_row, block), jnp.int32),
        in_specs=[anywhere] * n_col,
        out_specs=vmem,
        scratch_shapes=[pltpu.VMEM((n_col, 16, block), jnp.bfloat16), pltpu.SemaphoreType.DMA((n_col,))],
        name="keys",
    )(*hams)
    results = x_cols.shape[3] * x_cols.shape[4]
    halves = jax.ShapeDtypeStruct((2, results, block, block), jnp.bfloat16)
    pairs = pl.pallas_call(
        pair_kernel,
        out_shape=jax.ShapeDtypeStruct((512,), jnp.int32),
        in_specs=[smem] * 4,
        out_specs=smem,
        scratch_shapes=[pltpu.SMEM((n_depth * results,), jnp.int32)],
        name="pairs",
    )(where, ham_keys, it_keys, aim_keys)
    whole = jax.ShapeDtypeStruct((results, block, block), jnp.bfloat16)
    sent_on, sent_keep, kept = pl.pallas_call(
        product_kernel,
        out_shape=(whole, whole, halves),
        in_specs=[smem] + [anywhere] * 9,
        out_specs=(vmem,) * 3,
        scratch_shapes=[
            pltpu.VMEM((n_depth * results, block, block), jnp.float32),
            pltpu.VMEM((WINDOW, block, block), jnp.bfloat16),
            pltpu.VMEM((WINDOW, block, block), jnp.bfloat16),
            pltpu.SemaphoreType.DMA((WINDOW,)),
            pltpu.SemaphoreType.DMA((WINDOW,)),
        ],
        compiler_params=pltpu.CompilerParams(vmem_limit_bytes=24 << 20),
        name="products",
    )(*[pltpu.with_memory_space_constraint(x, pltpu.HBM) for x in (pairs, iterate)], *hams)
    to_core = [(d, d ^ 1) for d in range(n_depth)]
    near_on = lax.ppermute(sent_on, "depth", to_core)
    near_keep = lax.ppermute(sent_keep, "depth", to_core)
    onward = (kept[0].astype(jnp.float32) + near_on.astype(jnp.float32)).astype(jnp.bfloat16)
    onward, kept = lax.optimization_barrier((onward, kept))
    far = lax.ppermute(onward, "depth", [(d, d ^ 2) for d in range(n_depth)])
    prior = previous.reshape(results, block, block).astype(jnp.float32)
    live = x_flags.reshape(results, 1, 1).astype(jnp.float32)
    base = 2.0 * (kept[1].astype(jnp.float32) + near_keep.astype(jnp.float32)) - prior
    base = lax.optimization_barrier(base)
    result = (base + 2.0 * far.astype(jnp.float32)) * live
    return result.astype(jnp.bfloat16).reshape(previous.shape)


def solution(mesh):
    placed = (
        P("row", "col", "depth", None, None, None),
        P("row", "col", "depth", None),
        P("row", "col", "depth", None),
        P("row", "col", "depth", None),
        P("row", "depth", "col", None, None, None, None),
        P("row", "depth", "col", None, None),
        P("row", "depth", "col", None, None),
        P("row", "depth", "col", None, None, None, None),
    )
    return jax.shard_map(
        body,
        mesh=mesh,
        in_specs=placed,
        out_specs=P("row", "depth", "col", None, None, None, None),
        check_vma=False,
    )
```

```python
import jax
import jax.numpy as jnp
from jax import lax
from jax.experimental import pallas as pl
from jax.experimental.pallas import tpu as pltpu
from jax.sharding import PartitionSpec as P

WINDOW = 16


def key_kernel(*refs):
    hams, (keys, slab, sem) = refs[:8], refs[8:]
    tail = slab.shape[1]
    copies = [
        pltpu.make_async_copy(ham.at[pl.ds(ham.shape[0] - tail, tail)], slab.at[k], sem.at[k])
        for k, ham in enumerate(hams)
    ]
    for copy in copies:
        copy.start()
    for k, copy in enumerate(copies):
        copy.wait()
        held = slab[k].astype(jnp.float32)
        for t in range(2):
            row, col, flag = (held[3 * t + i : 3 * t + i + 1] for i in range(3))
            place = jnp.where(flag > 0, row * 8 + col, -1.0)
            keys[2 * k + t : 2 * k + t + 1] = place.astype(jnp.int32)


def pair_kernel(where, ham, iterate, aim, pairs, touched):
    def untouch(at, carry):
        touched[at] = 0
        return carry

    lax.fori_loop(0, aim.shape[0], untouch, 0)
    pieces = ham.shape[0]
    slots = 12
    per_col = pieces // 8
    width = iterate.shape[1]
    near = where[0] // 4
    step = where[0] % 4

    def one_tile(tile, count):
        array = tile // per_col
        col = ((array // 4) ^ near) * 4 + (step - array % 4 + 4) % 4
        piece = col * per_col + tile % per_col
        base = tile * slots + piece * width * 256

        def live(state):
            slot, _ = state
            return (slot < slots) & (ham[tile, slot] >= 0)

        def one_slot(state):
            slot, count = state
            key = ham[tile, slot]
            row = key // 8
            inner = key % 8
            for w in range(2):
                there = iterate[piece, inner * 2 + w]
                for v in range(2):
                    goal = row * 2 + v
                    match = (aim[goal] == there).astype(jnp.int32)
                    seen = touched[goal]
                    pairs[count] = base + slot + (inner * 2 + w) * 256 + (goal + 64 * seen) * 65536
                    touched[goal] = seen | match
                    count = count + match
            return slot + 1, count

        return lax.while_loop(live, one_slot, (jnp.int32(0), count))[1]

    pairs[pairs.shape[0] - 1] = lax.fori_loop(0, pieces, one_tile, jnp.int32(0))
    pairs[pairs.shape[0] - 2] = where[1]


def product_kernel(pairs, iterate, *rest):
    hams, (sent, kept, total, ham_buf, it_buf, ham_sem, it_sem) = rest[:8], rest[8:]
    size = ham_buf.shape[1]
    slots = hams[0].shape[0] // size
    count = pairs[pairs.shape[0] - 1]

    def start(at):
        code = pairs[at]
        ham_at = code % 256
        slot = at % WINDOW
        rows = pl.ds(pl.multiple_of((ham_at % slots) * size, size), size)
        for k, ham in enumerate(hams):

            @pl.when(ham_at // slots == k)
            def _():
                pltpu.make_async_copy(ham.at[rows], ham_buf.at[slot], ham_sem.at[slot]).start()

        pltpu.make_async_copy(iterate.at[(code // 256) % 256], it_buf.at[slot], it_sem.at[slot]).start()

    def first(at, carry):
        start(at)
        return carry

    lax.fori_loop(0, jnp.minimum(count, WINDOW), first, 0)

    half = sent.shape[1]
    depth = pairs[pairs.shape[0] - 2]
    core = depth % 2
    high = depth // 2

    def clear(at, carry):
        for part in range(2):
            sent[part, at] = jnp.zeros(sent.shape[2:], sent.dtype)
            kept[part, at] = jnp.zeros(kept.shape[2:], kept.dtype)
        return carry

    lax.fori_loop(0, half, clear, 0, unroll=4)

    def multiply(at, carry):
        slot = at % WINDOW
        pltpu.make_async_copy(hams[0].at[pl.ds(0, size)], ham_buf.at[slot], ham_sem.at[slot]).wait()
        pltpu.make_async_copy(iterate.at[0], it_buf.at[slot], it_sem.at[slot]).wait()
        goal = pairs[at] // 65536
        seen = goal >= 64
        goal = goal % 64
        product = jnp.dot(ham_buf[slot], it_buf[slot], preferred_element_type=jnp.float32)
        product = jnp.where(seen, total[goal], 0.0) + product
        total[goal] = product
        owner = goal // half
        part = (owner // 2 == high).astype(jnp.int32)

        @pl.when(owner % 2 == core)
        def _():
            kept[part, goal % half] = product.astype(kept.dtype)

        @pl.when(owner % 2 != core)
        def _():
            sent[part, goal % half] = product.astype(sent.dtype)

        @pl.when(at + WINDOW < count)
        def _():
            start(at + WINDOW)

        return carry

    lax.fori_loop(0, count, multiply, 0)


def body(h_blocks, h_rows, h_cols, h_flags, x_blocks, x_cols, x_flags, previous):
    block = x_blocks.shape[-1]
    n_row, n_col, n_depth = lax.axis_size("row"), lax.axis_size("col"), lax.axis_size("depth")
    where = jnp.stack([lax.axis_index("col"), lax.axis_index("depth")]).astype(jnp.int32)
    iterate = lax.all_gather(x_blocks[0, 0, 0], "row", axis=0)
    iterate = iterate.reshape(-1, block, block)
    it_ints = jnp.concatenate([x_cols, x_flags], axis=2)
    aim_ints = lax.all_gather(it_ints, "depth", axis=1, tiled=True)
    slots = h_rows.shape[-1]
    ham_ints = jnp.concatenate([h_rows, h_cols, h_flags], axis=2).reshape(-1, slots)
    ham_ints = ham_ints.astype(jnp.bfloat16)
    ham_ints = jnp.pad(ham_ints, ((0, 16 - ham_ints.shape[0]), (0, block - slots)))
    mine = jnp.concatenate([h_blocks.reshape(-1, block), ham_ints], axis=0)

    def send(source, flip, step):
        route = [(c, ((c // 4) ^ flip) * 4 + (c % 4 + step) % 4) for c in range(n_col)]
        return lax.ppermute(source, "col", route)

    hams = [mine] + [None] * (n_col - 1)
    for flip, step in ((0, 1), (0, 3)):
        hams[flip * 4 + step] = send(mine, flip, step)
    crossing, aim_ints = lax.optimization_barrier((mine, aim_ints))
    for flip, step in ((1, 0), (1, 2), (1, 1)):
        hams[flip * 4 + step] = send(crossing, flip, step)
    hams[1], crossing = lax.optimization_barrier((hams[1], crossing))
    hams[7] = send(crossing, 1, 3)
    hams[3], crossing, it_ints = lax.optimization_barrier((hams[3], crossing, it_ints))
    hams[2] = send(crossing, 0, 2)
    it_ints = lax.all_gather(it_ints, "row", axis=0, tiled=True)
    hams = [pltpu.with_memory_space_constraint(ham, pltpu.HBM) for ham in hams]
    it_keys = jnp.where(it_ints[:, 0, 1] > 0, it_ints[:, 0, 0], -1).reshape(n_row, -1)
    aim_keys = jnp.where(aim_ints[0, :, 1] > 0, aim_ints[0, :, 0], -2).reshape(-1)
    smem = pl.BlockSpec(memory_space=pltpu.SMEM)
    anywhere = pl.BlockSpec(memory_space=pl.ANY)
    vmem = pl.BlockSpec(memory_space=pltpu.VMEM)
    ham_keys = pl.pallas_call(
        key_kernel,
        out_shape=jax.ShapeDtypeStruct((n_row, block), jnp.int32),
        in_specs=[anywhere] * n_col,
        out_specs=vmem,
        scratch_shapes=[pltpu.VMEM((n_col, 16, block), jnp.bfloat16), pltpu.SemaphoreType.DMA((n_col,))],
        name="keys",
    )(*hams)
    results = x_cols.shape[3] * x_cols.shape[4]
    halves = jax.ShapeDtypeStruct((2, results, block, block), jnp.bfloat16)
    pairs = pl.pallas_call(
        pair_kernel,
        out_shape=jax.ShapeDtypeStruct((512,), jnp.int32),
        in_specs=[smem] * 4,
        out_specs=smem,
        scratch_shapes=[pltpu.SMEM((n_depth * results,), jnp.int32)],
        name="pairs",
    )(where, ham_keys, it_keys, aim_keys)
    sent, kept = pl.pallas_call(
        product_kernel,
        out_shape=(halves,) * 2,
        in_specs=[smem] + [anywhere] * 9,
        out_specs=(vmem,) * 2,
        scratch_shapes=[
            pltpu.VMEM((n_depth * results, block, block), jnp.float32),
            pltpu.VMEM((WINDOW, block, block), jnp.bfloat16),
            pltpu.VMEM((WINDOW, block, block), jnp.bfloat16),
            pltpu.SemaphoreType.DMA((WINDOW,)),
            pltpu.SemaphoreType.DMA((WINDOW,)),
        ],
        compiler_params=pltpu.CompilerParams(vmem_limit_bytes=24 << 20),
        name="products",
    )(*[pltpu.with_memory_space_constraint(x, pltpu.HBM) for x in (pairs, iterate)], *hams)
    near = lax.ppermute(sent, "depth", [(d, d ^ 1) for d in range(n_depth)])
    onward = (kept[0].astype(jnp.float32) + near[0].astype(jnp.float32)).astype(jnp.bfloat16)
    prior = previous.reshape(results, block, block).astype(jnp.float32)
    live = x_flags.reshape(results, 1, 1).astype(jnp.float32)
    base = 2.0 * (kept[1].astype(jnp.float32) + near[1].astype(jnp.float32)) - prior
    onward, base = lax.optimization_barrier((onward, base))
    far = lax.ppermute(onward, "depth", [(d, d ^ 2) for d in range(n_depth)])
    result = (base + 2.0 * far.astype(jnp.float32)) * live
    return result.astype(jnp.bfloat16).reshape(previous.shape)


def solution(mesh):
    placed = (
        P("row", "col", "depth", None, None, None),
        P("row", "col", "depth", None),
        P("row", "col", "depth", None),
        P("row", "col", "depth", None),
        P("row", "depth", "col", None, None, None, None),
        P("row", "depth", "col", None, None),
        P("row", "depth", "col", None, None),
        P("row", "depth", "col", None, None, None, None),
    )
    return jax.shard_map(
        body,
        mesh=mesh,
        in_specs=placed,
        out_specs=P("row", "depth", "col", None, None, None, None),
        check_vma=False,
    )
```
